512 devices in a mesh: seq: 128 (over z, x, core), tp: 4 (over y).
Axes of the slice: x: 4, y: 4, z: 16, core: 2. Of those that a mesh axis runs over, the one named last changes fastest.
Arguments:
- tokens: bfloat16 [32768, 2048], P('seq'), may hold values from -6 to 6
- norm_gain: float32 [2048], replicated, may hold values from 0.5 to 1.5
- q_gain: float32 [64], replicated, may hold values from 0.5 to 10
- k_gain: float32 [64], replicated, may hold values from 0.5 to 10
- w_query: bfloat16 [2048, 1280], P(None, 'tp'), may hold values from -0.125 to 0.125
- w_keyval: bfloat16 [2048, 640], P('tp'), may hold values from -0.125 to 0.125
- w_out: bfloat16 [1280, 2048], P('tp'), may hold values from -0.15625 to 0.15625
- lengths: int32 [64], replicated, may hold values from 1 to 8192, 32768 in all
- cache_place: int32 [32768, 2], P('seq'), may hold values from 0 to 255, as said below
Outputs:
- hidden: bfloat16 [32768, 2048], P(('seq', 'tp'))
- cache: bfloat16 [32768, 640], P('seq', 'tp')
The draws below stay inside these ranges and needn't reach their ends.
Inputs may be any that keep to these rules, and one draw needn't show every extreme that they name: `cache_place`: column 0 is the owner index of seq and column 1 the row there. The tokens of one index of seq go in groups of exactly 4 to 64 different owners, and each owner's 256 rows are each named once.
All inputs are finite; a program needn't handle non-finite values.
Results may differ from the reference program's by a relative error of at most 0.015.
The reference program's roundings to bfloat16 on the way (of `normed`, `query`, `keys`, `values`, `weights` and `attended`) count: a program that leaves them out, or rounds other values in their place, can miss the bound.
Values may be sent and summed in bfloat16 or wider, within the bound.
A program may use at most 64 MiB of HBM per device.

```python
import math
import jax
import jax.numpy as jnp
import numpy as np
from jax import lax

D = 2048
QH = 20
KVH = 5
HD = 64
TOK_DEV = 256
GROUP = 4
KVW = 640
TOKENS = 32768
SPAN = 32
MAXLEN = 8192
NSEG = 64
CAP = 4


def draw_q_gain(key, part):
    gain_key = jax.random.fold_in(key, 41)
    drawn = 1.0 + 0.18 * jnp.clip(jax.random.normal(gain_key, (HD,), jnp.float32), -2.5, 2.5)
    return drawn.astype(jnp.float32)


def draw_k_gain(key, part):
    gain_key = jax.random.fold_in(key, 53)
    drawn = 1.0 + 0.18 * jnp.clip(jax.random.normal(gain_key, (HD,), jnp.float32), -2.5, 2.5)
    return drawn.astype(jnp.float32)


def draw_cache_place(key, part):
    devices_seq = TOKENS // TOK_DEV
    groups = TOK_DEV // CAP
    half_way = devices_seq // 2
    key_offset = jax.random.fold_in(key, 11)
    key_local = jax.random.fold_in(key, 23)
    key_rows = jax.random.fold_in(key, 37)
    others = jax.random.permutation(key_offset, devices_seq - 1).astype(jnp.int32)
    others = others + (others >= half_way).astype(jnp.int32)
    offsets = jnp.concatenate([jnp.full((1,), half_way, jnp.int32), others[:groups - 1]], axis=0)
    local_keys = jax.random.split(key_local, devices_seq)
    orders = jax.vmap(lambda one_key: jax.random.permutation(one_key, TOK_DEV))(local_keys).astype(jnp.int32)
    group_of = orders // CAP
    within = orders % CAP
    source = jnp.arange(devices_seq, dtype=jnp.int32)[:, None]
    owner_dev = (offsets[group_of] + source) % devices_seq
    base_row = group_of * CAP + within
    row_keys = jax.random.split(key_rows, devices_seq)
    row_orders = jax.vmap(lambda one_key: jax.random.permutation(one_key, TOK_DEV))(row_keys).astype(jnp.int32)
    slot_index = row_orders[owner_dev, base_row]
    return jnp.stack([owner_dev, slot_index], axis=-1).reshape(TOKENS, 2).astype(jnp.int32)


def block_levels(stream_key, shape, pieces, low, largest):
    level = 1.0
    for dim, parts in pieces:
        heights = jax.random.uniform(jax.random.fold_in(jax.random.fold_in(stream_key, 6), dim), (parts,), jnp.float32, low / len(pieces), largest / len(pieces))
        level = level * jnp.repeat(jnp.exp(heights), shape[dim] // parts).reshape((-1,) + (1,) * (len(shape) - 1 - dim))
    return level


def split_up(count, total, most, lean):
    portions = [(1 << 20) // math.isqrt(grade ** lean) + 1 for grade in range(2, count + 1)]
    rest, holding = total - most - (count - 1), [1] * (count - 1)
    while rest > 0:
        free = [i for i in range(count - 1) if holding[i] < most]
        pool, left = sum([portions[i] for i in free]), rest
        for i in free:
            more = min(most - holding[i], max(1, left * portions[i] // pool), rest)
            holding[i] = holding[i] + more
            rest = rest - more
    return np.array([most] + holding)


def ragged_sizes(rng, number_of, total, most, lean):
    if number_of == 2:
        one = jax.random.randint(rng, (), max(1, total - most), min(most, total - 1) + 1)
        return jnp.stack([one, total - one])
    sizes = jnp.asarray(split_up(number_of, total, most, lean), jnp.int32)
    twos = (number_of - 1) // 2
    donor, receiver = sizes[1:1 + 2 * twos:2], sizes[2:2 + 2 * twos:2]
    margin = jnp.minimum(donor - 1, most - receiver)
    shifted = jax.random.randint(jax.random.fold_in(rng, 1), (twos,), 0, 1 << 20) % (margin + 1)
    sizes = sizes.at[1:1 + 2 * twos:2].set(donor - shifted).at[2:2 + 2 * twos:2].set(receiver + shifted)
    return sizes[jax.random.permutation(jax.random.fold_in(rng, 2), number_of)]


def centred(key, shape, width, reach, cuts=(), held_as=jnp.bfloat16):
    loudness = block_levels(key, shape, cuts, -0.22, 0.18) if cuts else 1.0
    result = jax.random.normal(key, shape, jnp.float32) * width * loudness
    return jnp.minimum(jnp.maximum(result, -reach), reach).astype(held_as)


def setup_inputs(seed: int = 0) -> dict:
    key_list = jax.random.split(jax.random.key(seed), 10)
    tokens = centred(key_list[0], (TOKENS, D), 1.0, 6.0, ((0, 128),))
    norm_gain = jnp.clip(1.0 + 0.1 * jax.random.normal(key_list[1], (D,), jnp.float32), 0.5, 1.5)
    q_gain = draw_q_gain(jax.random.fold_in(key_list[9], 71), 0)
    k_gain = draw_k_gain(jax.random.fold_in(key_list[9], 71), 0)
    w_query = centred(key_list[4], (D, QH * HD), D ** -0.5, 0.125, ((1, 4),))
    w_keyval = centred(key_list[5], (D, KVW), D ** -0.5, 0.125, ((0, 4),))
    w_out = centred(key_list[6], (QH * HD, D), (QH * HD) ** -0.5, 0.15625, ((0, 4),))
    lengths = ragged_sizes(key_list[7], NSEG, TOKENS, MAXLEN, 2).astype(jnp.int32)
    cache_place = draw_cache_place(jax.random.fold_in(key_list[9], 71), 0)
    return dict(tokens=tokens, norm_gain=norm_gain, q_gain=q_gain, k_gain=k_gain, w_query=w_query, w_keyval=w_keyval, w_out=w_out, lengths=lengths, cache_place=cache_place)


epsilon = 1e-06
rope_base = 10000.0
masked_value = -1e+30

def rms_norm(vector, scale_gain):
    return vector * lax.rsqrt(lax.optimization_barrier(jnp.mean(vector * vector, axis=-1, keepdims=True)) + epsilon) * scale_gain

def rotate(vector, position):
    half_dim = vector.shape[-1] // 2
    frequency = rope_base ** (-(jnp.arange(half_dim, dtype=jnp.float32) * 2.0) / vector.shape[-1])
    angles = position.astype(jnp.float32)[:, None] * frequency[None, :]
    cosine = jnp.cos(angles)[:, None, :]
    sine = jnp.sin(angles)[:, None, :]
    first_half = vector[..., :half_dim]
    second_half = vector[..., half_dim:]
    return jnp.concatenate([first_half * cosine - second_half * sine, second_half * cosine + first_half * sine], axis=-1)

def segment_info(lengths, indices):
    segment_ends = jnp.cumsum(lengths).astype(jnp.int32)
    segment = lax.optimization_barrier(jnp.sum((segment_ends[None, :] <= indices[:, None]).astype(jnp.int32), axis=1))
    starts = segment_ends - lengths
    onehot = segment[:, None] == jnp.arange(lengths.shape[0], dtype=jnp.int32)[None, :]
    first_token = lax.optimization_barrier(jnp.sum(jnp.where(onehot, starts[None, :], 0), axis=1)).astype(jnp.int32)
    return (segment, indices - first_token)

def reference(tokens, norm_gain, q_gain, k_gain, w_query, w_keyval, w_out, lengths, cache_place):
    total_rows = tokens.shape[0]
    indices = jnp.arange(total_rows, dtype=jnp.int32)
    segment, position = segment_info(lengths, indices)
    residual = tokens.astype(jnp.float32)
    normed = rms_norm(residual, norm_gain).astype(jnp.bfloat16)
    query = jnp.dot(normed, w_query, preferred_element_type=jnp.float32).reshape(total_rows, QH, HD)
    query = rotate(rms_norm(query, q_gain), position).astype(jnp.bfloat16)
    keyval = jnp.dot(normed, w_keyval, preferred_element_type=jnp.float32)
    half_cols = KVH * HD
    keys = rotate(rms_norm(keyval[:, :half_cols].reshape(total_rows, KVH, HD), k_gain), position).astype(jnp.bfloat16)
    values = keyval[:, half_cols:].astype(jnp.bfloat16).reshape(total_rows, KVH, HD)
    entries = jnp.concatenate([keys.reshape(total_rows, half_cols), values.reshape(total_rows, half_cols)], axis=1)
    target = (cache_place[:, 0] * TOK_DEV + cache_place[:, 1]).astype(jnp.int32)
    cache = jnp.zeros((total_rows, 2 * half_cols), jnp.bfloat16).at[target].set(entries)
    front = SPAN * TOK_DEV
    window_rows = front + TOK_DEV
    keys_pad = jnp.pad(keys, ((front, 0), (0, 0), (0, 0)))
    values_pad = jnp.pad(values, ((front, 0), (0, 0), (0, 0)))
    segment_pad = jnp.pad(segment, (front, 0), constant_values=-1)
    scale = 1.0 / HD ** 0.5

    def one_block(block_id):
        begin = (block_id * TOK_DEV).astype(jnp.int32)
        q_rows = lax.dynamic_slice_in_dim(query, begin, TOK_DEV, 0).astype(jnp.float32)
        q_segment = lax.dynamic_slice_in_dim(segment, begin, TOK_DEV, 0)
        q_index = begin + jnp.arange(TOK_DEV, dtype=jnp.int32)
        k_rows = jnp.repeat(lax.dynamic_slice_in_dim(keys_pad, begin, window_rows, 0).astype(jnp.float32), GROUP, axis=1)
        v_rows = jnp.repeat(lax.dynamic_slice_in_dim(values_pad, begin, window_rows, 0).astype(jnp.float32), GROUP, axis=1)
        k_segment = lax.dynamic_slice_in_dim(segment_pad, begin, window_rows, 0)
        k_index = begin - front + jnp.arange(window_rows, dtype=jnp.int32)
        allowed = (k_index[None, :] <= q_index[:, None]) & (k_segment[None, :] == q_segment[:, None])
        scores = jnp.einsum('qhd,khd->hqk', q_rows, k_rows) * scale
        scores = jnp.where(allowed[None], scores, masked_value)
        top_score = lax.optimization_barrier(jnp.max(scores, axis=-1, keepdims=True))
        weights = jnp.where(allowed[None], jnp.exp(scores - top_score), 0.0)
        total_weight = lax.optimization_barrier(jnp.sum(weights, axis=-1))
        rounded = weights.astype(jnp.bfloat16).astype(jnp.float32)
        mixed = jnp.einsum('hqk,khd->qhd', rounded, v_rows) / jnp.transpose(total_weight)[:, :, None]
        return mixed.reshape(TOK_DEV, QH * HD).astype(jnp.bfloat16)
    attended = lax.map(one_block, jnp.arange(total_rows // TOK_DEV, dtype=jnp.int32)).reshape(total_rows, QH * HD)
    hidden = (jnp.dot(attended, w_out, preferred_element_type=jnp.float32) + residual).astype(jnp.bfloat16)
    return (hidden, cache)
```

```python
import functools
import numpy as np
import jax
import jax.numpy as jnp
from jax import lax
from jax.experimental import pallas as pl
from jax.experimental.pallas import tpu as pltpu
from jax.sharding import PartitionSpec as P

EPS = 1e-06
BASE = 10000.0
FAR = 16384.0
MESH = pl.DeviceIdType.MESH
F32 = jnp.float32
BF16 = jnp.bfloat16
CORES = 2
XN = 4
PLANE = XN * CORES
BACK = 4
TP = 4


def dot(a, b, ca=1, cb=0):
    return lax.dot_general(a, b, (((ca,), (cb,)), ((), ())), preferred_element_type=F32)


def iota(shape, axis):
    return lax.broadcasted_iota(jnp.int32, shape, axis)


def kernel(
    zn, tokens, ngain, qgain, kgain, freq, lens, place, wq, wkv, wo,
    hidden, cache,
    wkvb, wob, normed, kvt, qext, kv, kmask, mrun, lrun, acc, att, attr, attf,
    pack, mid, midp, fin, loc, wss, wrs, kss, krs, krs2, css, crs, dss, drs, ess, ers,
):
    rows, width = tokens.shape
    hd = qgain.shape[1]
    half = hd // 2
    nseg = lens.shape[1]
    ql = wq.shape[1] // hd
    kvw = wkv.shape[1]
    keyw = kvw // 2
    kvh = keyw // hd
    group = ql * TP // kvh
    cols = kvw // TP
    s = lax.axis_index("seq")
    t = lax.axis_index("tp")
    z = s // PLANE
    p = s % PLANE
    x = p // CORES
    c = p % CORES
    tm, tq, t2 = (t + TP - 1) % TP, (t + 1) % TP, (t + 2) % TP
    xm, xq, x2 = (x + XN - 1) % XN, (x + 1) % XN, (x + 2) % XN
    pm, pq, p2 = xm * CORES + c, xq * CORES + c, x2 * CORES + c
    po = x * CORES + 1 - c
    zq = (z + 1) % zn
    plane0 = z * PLANE
    other = (plane0 + po, t)
    xplus = (plane0 + pq, t)
    xminus = (plane0 + pm, t)
    zplus = (zq * PLANE + p, t)

    def remote(src, dst, ss, rs, dev):
        return pltpu.make_async_remote_copy(
            src_ref=src, dst_ref=dst, send_sem=ss, recv_sem=rs, device_id=dev, device_id_type=MESH
        )

    krows = wkv.shape[0]
    orows = wo.shape[0]
    cp_kv = pltpu.make_async_copy(wkv, wkvb.at[pl.ds(t * krows, krows), :], loc.at[0])
    cp_o = pltpu.make_async_copy(wo, wob.at[pl.ds(t * orows, orows), :], loc.at[1])
    cp_kv.start()
    cp_o.start()

    barrier = pltpu.get_barrier_semaphore()
    for i in range(1, TP):
        pl.semaphore_signal(barrier, inc=1, device_id=(s, (t + i) % TP), device_id_type=MESH)
    for i in range(1, PLANE):
        pl.semaphore_signal(
            barrier, inc=1, device_id=(plane0 + (p + i) % PLANE, t), device_id_type=MESH
        )

    def greet(i, carry):
        pl.semaphore_signal(
            barrier, inc=1, device_id=(((z + i) % zn) * PLANE + p, t), device_id_type=MESH
        )
        return carry

    lax.fori_loop(1, zn, greet, 0)
    pl.semaphore_wait(barrier, (TP - 1) + (PLANE - 1) + (zn - 1))

    def piece(w, ti, ci, part, parts):
        buf, n = (wkvb, krows) if w == 0 else (wob, orows)
        h = n // 2
        m = h // parts
        start = pl.multiple_of(ti * n + ci * h + part * m, 16)
        return buf.at[pl.ds(start, m), :]

    def wcopy(w, k, ti, part, parts, dev, r):
        ref = piece(w, ti, c, part, parts)
        return remote(ref, ref, wss.at[w, k], wrs.at[w, r], dev)

    def wwait(w, r, ti, ci, part, parts):
        ref = piece(w, ti, ci, part, parts)
        remote(ref, ref, wss.at[w, r], wrs.at[w, r], other).wait_recv()

    def wsend(w, k):
        ti, part, parts, dev = (
            (t, 0, 1, (s, tq)),
            (t, 0, 1, (s, tm)),
            (tm, 0, 2, (s, tq)),
            (tq, 1, 2, (s, tm)),
            (tm, 0, 1, other),
            (tq, 0, 1, other),
            (t2, 0, 1, other),
        )[k]
        return wcopy(w, k, ti, part, parts, dev, k)

    def wfirst(w):
        wsend(w, 0).start()
        wsend(w, 1).start()

    def wrelay(w):
        wwait(w, 0, tm, c, 0, 1)
        wsend(w, 2).start()
        wsend(w, 4).start()
        wwait(w, 1, tq, c, 0, 1)
        wsend(w, 3).start()
        wsend(w, 5).start()

    def wlast(w):
        wwait(w, 2, t2, c, 0, 2)
        wwait(w, 3, t2, c, 1, 2)
        wsend(w, 6).start()

    def wdone(w):
        wwait(w, 4, tm, 1 - c, 0, 1)
        wwait(w, 5, tq, 1 - c, 0, 1)
        wwait(w, 6, t2, 1 - c, 0, 1)

    cp_kv.wait()
    wfirst(0)

    step = 64

    def norm_rows(i, carry):
        r = pl.ds(pl.multiple_of(i * step, step), step)
        v = tokens[r, :].astype(F32)
        ms = jnp.mean(v * v, axis=1, keepdims=True)
        normed[r, :] = (v * lax.rsqrt(ms + EPS) * ngain[...]).astype(BF16)
        return carry

    lax.fori_loop(0, rows // step, norm_rows, 0)

    lens_f = lens[...].astype(F32)
    e0 = iota((nseg, nseg), 0)
    e1 = iota((nseg, nseg), 1)
    lens_b = jnp.broadcast_to(lens_f, (nseg, nseg))
    ends_col = jnp.sum(jnp.where(e1 <= e0, lens_b, 0.0), axis=1, keepdims=True)
    lens_col = jnp.sum(jnp.where(e1 == e0, lens_b, 0.0), axis=1, keepdims=True)
    starts_col = ends_col - lens_col
    f0 = iota((nseg, 128), 0)
    f1 = iota((nseg, 128), 1)
    ends_row = jnp.sum(jnp.where(f0 <= f1, lens_col, 0.0), axis=0, keepdims=True)
    starts_row = jnp.sum(jnp.where(f0 < f1, lens_col, 0.0), axis=0, keepdims=True)
    q_idx = (iota((1, rows), 1) + s * rows).astype(F32)
    inside = (starts_col <= q_idx) & (q_idx < ends_col)
    onehot_q = jnp.where(inside, 1.0, 0.0)
    first = jnp.sum(jnp.where(inside, starts_col, 0.0), axis=0, keepdims=True)
    angle = (q_idx - first) * freq[...]
    cosine = jnp.cos(angle)
    sine = jnp.sin(angle)
    g0 = iota((hd, hd), 0)
    g1 = iota((hd, hd), 1)
    qg = jnp.sum(jnp.where(g0 == g1, qgain[...], 0.0), axis=1, keepdims=True)
    kg = jnp.sum(jnp.where(g0 == g1, kgain[...], 0.0), axis=1, keepdims=True)

    def norm_rotate(h, gain):
        ms = jnp.mean(h * h, axis=0, keepdims=True)
        h = h * lax.rsqrt(ms + EPS) * gain
        u, w = h[:half], h[half:]
        return jnp.concatenate([u * cosine - w * sine, w * cosine + u * sine], axis=0)

    qt = jnp.transpose(dot(normed[...], wq[...]))
    head0 = (t * ql) // group

    def pick(j):
        return (t * ql + j) // group - head0

    tail = jnp.concatenate([onehot_q, jnp.zeros((128 - nseg, rows), F32)], axis=0).astype(BF16)
    for j in range(ql):
        rot = norm_rotate(qt[j * hd : (j + 1) * hd], qg)
        second = (pick(j) == 1).astype(F32)
        qext[j, 0:hd, :] = (rot * (1.0 - second)).astype(BF16)
        qext[j, hd : 2 * hd, :] = (rot * second).astype(BF16)
        qext[j, 2 * hd :, :] = tail

    wrelay(0)
    cp_o.wait()
    wlast(0)
    wfirst(1)
    wdone(0)
    kvf = jnp.transpose(dot(normed[...], wkvb[...]))
    for j in range(kvh):
        kvt[j * hd : (j + 1) * hd, :] = norm_rotate(kvf[j * hd : (j + 1) * hd], kg).astype(BF16)
    kvt[keyw:kvw, :] = kvf[keyw:kvw].astype(BF16)
    kt = kvt[pl.ds(pl.multiple_of(head0 * hd, hd), 2 * hd), :]
    vt = kvt[pl.ds(pl.multiple_of(keyw + head0 * hd, hd), 2 * hd), :]
    kv[0, p, 0:rows, :] = jnp.transpose(kt.astype(F32)).astype(BF16)
    kv[0, p, rows : rows + 128, :] = vt[:, 0:128]
    kv[0, p, rows + 128 : rows + 256, :] = vt[:, 128:256]

    def kcopy(k, d):
        def whole(q):
            return kv.at[d, q]

        if k == 0:
            return remote(whole(p), kv.at[d + 1, p], kss.at[d, 0], krs.at[d + 1, p], zplus)
        if k == 1:
            return remote(whole(p), whole(p), kss.at[d, 1], krs.at[d, p], xplus)
        if k == 2:
            return remote(whole(p), whole(p), kss.at[d, 2], krs.at[d, p], xminus)
        if k == 3:
            return remote(whole(p), whole(p), kss.at[d, 3], krs.at[d, p], other)
        if k == 4:
            ref = kv.at[d, pm, pl.ds(0, rows), :]
            return remote(ref, ref, kss.at[d, 4], krs.at[d, pm], xplus)
        if k == 5:
            ref = kv.at[d, pq, pl.ds(rows, rows), :]
            return remote(ref, ref, kss.at[d, 5], krs2.at[d], xminus)
        q = (pm, pq, p2)[k - 6]
        return remote(whole(q), whole(q), kss.at[d, k], krs.at[d, q], other)

    def kwait(d, q):
        ref = kv.at[d, q]
        remote(ref, ref, kss.at[d, 0], krs.at[d, q], other).wait_recv()

    def own(d):
        for k in (1, 2, 3):
            kcopy(k, d).start()

    def arrive(d):
        kwait(d, p)

    def sides(d):
        kwait(d, pm)
        kcopy(4, d).start()
        kcopy(6, d).start()
        kwait(d, pq)
        kcopy(5, d).start()
        kcopy(7, d).start()

    def across(d):
        ref = kv.at[d, p2, pl.ds(0, rows), :]
        remote(ref, ref, kss.at[d, 4], krs.at[d, p2], other).wait_recv()
        ref = kv.at[d, p2, pl.ds(rows, rows), :]
        remote(ref, ref, kss.at[d, 5], krs2.at[d], other).wait_recv()
        kcopy(8, d).start()

    def mates(d):
        for i in range(XN):
            kwait(d, i * CORES + 1 - c)

    kcopy(0, 0).start()
    own(0)

    scale = float(1.0 / hd**0.5 * np.log2(np.e))

    def seg_mask(base):
        k_idx = (iota((rows, 128), 0) + base).astype(F32)
        outside = (k_idx < starts_row) | (k_idx >= ends_row)
        return jnp.where(outside, -FAR, 0.0).astype(BF16)

    causal = iota((rows, rows), 0) <= iota((rows, rows), 1)
    own_ext = jnp.concatenate([kv[0, p, 0:rows, :], seg_mask(s * rows)], axis=1)
    for j in range(ql):
        sc = jnp.where(causal, dot(own_ext, qext[j]), -FAR)
        m = jnp.max(sc, axis=0, keepdims=True)
        w = jnp.exp2((sc - m) * scale)
        mrun[j] = m
        lrun[j] = jnp.sum(w, axis=0, keepdims=True)
        acc[j] = dot(vt, w.astype(BF16))

    cap = pack.shape[0] // (zn * PLANE)
    owner_col = place[:, 0:1].astype(F32)
    placef = jnp.concatenate(
        [place[...].astype(F32), jnp.zeros((rows, 128 - place.shape[1]), F32)], axis=1
    )
    placet = jnp.transpose(placef)
    owner_row = placet[0:1, :]
    slot_row = placet[1:2, :]
    earlier = iota((rows, rows), 0) < iota((rows, rows), 1)
    rank = jnp.sum(
        jnp.where(earlier & (owner_col == owner_row), 1.0, 0.0), axis=0, keepdims=True
    )
    to_row = owner_row * cap + rank
    sel = jnp.where(iota((pack.shape[0], rows), 0).astype(F32) == to_row, 1.0, 0.0).astype(BF16)
    mine = kvt[pl.ds(pl.multiple_of(t * cols, 16), cols), :]
    extra = jnp.where(iota((pack.shape[1] - cols, rows), 0) == 0, slot_row + 1.0, 0.0)
    feats = jnp.concatenate([mine, extra.astype(BF16)], axis=0)
    pack[...] = dot(sel, feats, 1, 1).astype(BF16)
    zrows = PLANE * cap
    prows = zn * cap

    def zcopy(i):
        zt = (z + i) % zn
        return remote(
            pack.at[pl.ds(pl.multiple_of(zt * zrows, zrows), zrows), :],
            mid.at[pl.ds(pl.multiple_of(z * zrows, zrows), zrows), :],
            css.at[i], crs.at[z], (zt * PLANE + p, t),
        )

    def zstart(i, carry):
        zcopy(i).start()
        return carry

    def zwait(i, carry):
        zs = (z + i) % zn
        ref = mid.at[pl.ds(pl.multiple_of(zs * zrows, zrows), zrows), :]
        remote(ref, ref, css.at[i], crs.at[zs], other).wait_recv()
        return carry

    def pcopy(i):
        q = (p + i) % PLANE
        return remote(
            midp.at[pl.ds(pl.multiple_of(q * prows, prows), prows), :],
            fin.at[pl.ds(pl.multiple_of(p * prows, prows), prows), :],
            dss.at[i], drs.at[p], (plane0 + q, t),
        )

    lax.fori_loop(1, zn, zstart, 0)
    zown = pl.ds(pl.multiple_of(z * zrows, zrows), zrows)
    mid[zown, :] = pack[zown, :]

    def cache_second():
        lax.fori_loop(1, zn, zwait, 0)
        n = pack.shape[0]
        r0 = iota((n, n), 0)
        r1 = iota((n, n), 1)
        src = ((r0 % prows) // cap) * zrows + (r0 // prows) * cap + r0 % cap
        perm = jnp.where(r1 == src, 1.0, 0.0).astype(BF16)
        midp[...] = dot(perm, mid[...]).astype(BF16)
        for i in range(1, PLANE):
            pcopy(i).start()
        pown = pl.ds(pl.multiple_of(p * prows, prows), prows)
        fin[pown, :] = midp[pown, :]

    arrive(1)
    kcopy(0, 1).start()
    own(1)
    sides(0)
    arrive(2)
    kcopy(0, 2).start()
    own(2)
    sides(1)
    across(0)
    across(1)
    mates(0)

    sub = 2
    full = BACK * ql

    def turn(i, carry):
        d = 1 + i // ql
        j = i % ql

        def plane_of(q):
            return jnp.where((d == BACK) & (q < p), 0, d)

        @pl.when(j == 0)
        def _():
            mates(d)
            for q in range(PLANE):
                base = ((z - plane_of(q)) * PLANE + q) * rows
                kmask[q * rows : (q + 1) * rows, :] = seg_mask(base)

        qj = qext[j]
        m = mrun[j]
        l = lrun[j]
        a = acc[j]
        for b in range(0, PLANE, sub):
            qs = range(b, b + sub)
            ks = jnp.concatenate([kv[plane_of(q), q, 0:rows, :] for q in qs], axis=0)
            ext = jnp.concatenate([ks, kmask[b * rows : (b + sub) * rows, :]], axis=1)
            vs = jnp.concatenate(
                [
                    kv[plane_of(q), q, rows + o : rows + o + 128, :]
                    for q in qs
                    for o in (0, 128)
                ],
                axis=1,
            )
            sc = dot(ext, qj)
            mn = jnp.maximum(m, jnp.max(sc, axis=0, keepdims=True))
            w = jnp.exp2((sc - mn) * scale)
            al = jnp.exp2((m - mn) * scale)
            l = l * al + jnp.sum(w, axis=0, keepdims=True)
            a = a * al + dot(vs, w.astype(BF16))
            m = mn
        mrun[j] = m
        lrun[j] = l
        acc[j] = a

        @pl.when((j == 0) & (d + 2 <= BACK))
        def _():
            arrive(d + 2)

            @pl.when(d + 2 < BACK)
            def _():
                kcopy(0, d + 2).start()

            own(d + 2)

        @pl.when((j == 1) & (d < BACK))
        def _():
            sides(d + 1)

        @pl.when((j == 3) & (d < BACK))
        def _():
            across(d + 1)

        @pl.when(i == ql + 2)
        def _():
            wrelay(1)

        @pl.when(i == 3 * ql)
        def _():
            wlast(1)
            cache_second()

        return carry

    lax.fori_loop(0, full, turn, 0)

    for j in range(ql):
        o = acc[j, pl.ds(pl.multiple_of(pick(j) * hd, hd), hd), :] / lrun[j]
        att[:, j * hd : (j + 1) * hd] = jnp.transpose(o).astype(BF16)
    orow = rows // TP

    def acopy(i):
        ti = (t + i) % TP
        return remote(
            att.at[pl.ds(pl.multiple_of(ti * orow, orow), orow), :],
            attr.at[t], ess.at[i], ers.at[t], (s, ti),
        )

    for i in range(1, TP):
        acopy(i).start()
    attr[t] = att[pl.ds(pl.multiple_of(t * orow, orow), orow), :]

    for i in range(1, PLANE):
        q = (p + i) % PLANE
        ref = fin.at[pl.ds(pl.multiple_of(q * prows, prows), prows), :]
        remote(ref, ref, dss.at[i], drs.at[q], other).wait_recv()
    got = fin[...]
    slot_col = got[:, cols : cols + 1].astype(F32)
    n = pack.shape[0]
    put = jnp.where(slot_col == (iota((n, rows), 1) + 1).astype(F32), 1.0, 0.0).astype(BF16)
    cache[...] = dot(put, got, 0, 0)[:, 0:cols].astype(BF16)

    wdone(1)
    for i in range(1, TP):
        ti = (t + i) % TP
        remote(attr.at[ti], attr.at[ti], ess.at[i], ers.at[ti], other).wait_recv()
    for ti in range(TP):
        attf[:, ti * ql * hd : (ti + 1) * ql * hd] = attr[ti]
    resid = tokens[pl.ds(pl.multiple_of(t * orow, orow), orow), :].astype(F32)
    hidden[...] = (dot(attf[...], wob[...]) + resid).astype(BF16)

    for w in range(2):
        for k in range(7):
            wsend(w, k).wait_send()

    def kdone(d, carry):
        @pl.when(d < BACK)
        def _():
            kcopy(0, d).wait_send()

        for k in range(1, 9):
            kcopy(k, d).wait_send()
        return carry

    lax.fori_loop(0, BACK + 1, kdone, 0)

    def zdone(i, carry):
        zcopy(i).wait_send()
        return carry

    lax.fori_loop(1, zn, zdone, 0)
    for i in range(1, PLANE):
        pcopy(i).wait_send()
    for i in range(1, TP):
        acopy(i).wait_send()


def per_device(tokens, norm_gain, q_gain, k_gain, w_query, w_keyval, w_out, lengths, cache_place):
    rows, width = tokens.shape
    seqs = lax.axis_size("seq")
    zn = seqs // PLANE
    hd = q_gain.shape[0]
    kvw = w_keyval.shape[1]
    cols = kvw // TP
    ql = w_query.shape[1] // hd
    cap = CAPACITY
    freq = (BASE ** (-(np.arange(hd // 2, dtype=np.float64) * 2.0) / hd)).astype(np.float32)
    vm = pl.BlockSpec(memory_space=pltpu.VMEM)
    hbm = pl.BlockSpec(memory_space=pl.ANY)
    packed = (seqs * cap, 256)
    dma = pltpu.SemaphoreType.DMA
    return pl.pallas_call(
        functools.partial(kernel, zn),
        out_shape=(
            jax.ShapeDtypeStruct((rows // TP, width), BF16),
            jax.ShapeDtypeStruct((rows, cols), BF16),
        ),
        in_specs=[vm] * 8 + [hbm] * 2,
        out_specs=(vm, vm),
        scratch_shapes=[
            pltpu.VMEM((w_keyval.shape[0] * TP, kvw), BF16),
            pltpu.VMEM((w_out.shape[0] * TP, width), BF16),
            pltpu.VMEM((rows, width), BF16),
            pltpu.VMEM((kvw, rows), BF16),
            pltpu.VMEM((ql, 256, rows), BF16),
            pltpu.VMEM((BACK + 1, PLANE, 2 * rows, 128), BF16),
            pltpu.VMEM((PLANE * rows, 128), BF16),
            pltpu.VMEM((ql, 1, rows), F32),
            pltpu.VMEM((ql, 1, rows), F32),
            pltpu.VMEM((ql, 2 * hd, rows), F32),
            pltpu.VMEM((rows, ql * hd), BF16),
            pltpu.VMEM((TP, rows // TP, ql * hd), BF16),
            pltpu.VMEM((rows // TP, TP * ql * hd), BF16),
            pltpu.VMEM(packed, BF16),
            pltpu.VMEM(packed, BF16),
            pltpu.VMEM(packed, BF16),
            pltpu.VMEM(packed, BF16),
            dma((2,)),
            dma((2, 7)),
            dma((2, 7)),
            dma((BACK + 1, 9)),
            dma((BACK + 1, PLANE)),
            dma((BACK + 1,)),
            dma((zn,)),
            dma((zn,)),
            dma((PLANE,)),
            dma((PLANE,)),
            dma((TP,)),
            dma((TP,)),
        ],
        compiler_params=pltpu.CompilerParams(
            collective_id=0, has_side_effects=True, vmem_limit_bytes=56 << 20
        ),
        name="layer",
    )(
        tokens,
        norm_gain.reshape(1, width),
        q_gain.reshape(1, hd),
        k_gain.reshape(1, hd),
        jnp.asarray(freq.reshape(-1, 1)),
        lengths.reshape(1, -1),
        cache_place,
        w_query,
        w_keyval,
        w_out,
    )


CAPACITY = 4


def solution(mesh):
    placed = (
        P("seq", None),
        P(),
        P(),
        P(),
        P(None, "tp"),
        P("tp", None),
        P("tp", None),
        P(),
        P("seq", None),
    )
    return jax.shard_map(
        per_device,
        mesh=mesh,
        in_specs=placed,
        out_specs=(P(("seq", "tp"), None), P("seq", "tp")),
        check_vma=False,
    )
```

```python
import functools
import numpy as np
import jax
import jax.numpy as jnp
from jax import lax
from jax.experimental import pallas as pl
from jax.experimental.pallas import tpu as pltpu
from jax.sharding import PartitionSpec as P

EPS = 1e-06
BASE = 10000.0
FAR = 16384.0
MESH = pl.DeviceIdType.MESH
F32 = jnp.float32
BF16 = jnp.bfloat16
CORES = 2
XN = 4
PLANE = XN * CORES
BACK = 4
TP = 4


def dot(a, b, ca=1, cb=0):
    return lax.dot_general(a, b, (((ca,), (cb,)), ((), ())), preferred_element_type=F32)


def iota(shape, axis):
    return lax.broadcasted_iota(jnp.int32, shape, axis)


def kernel(
    zn, ngain, qgain, kgain, freq, lens, place, tokens_h, wq_h, wkv, wo,
    hidden, cache,
    tokens, wq, wkvb, wob, normed, kvt, qext, kv, mrun, lrun, acc, att, attr, attf,
    pack, mid, midp, fin, loc, wss, wrs, kss, krs, krs2, css, crs, dss, drs, ess, ers,
):
    rows, width = tokens.shape
    hd = qgain.shape[1]
    half = hd // 2
    nseg = lens.shape[1]
    ql = wq.shape[0] // hd
    kvw = wkv.shape[1]
    keyw = kvw // 2
    kvh = keyw // hd
    group = ql * TP // kvh
    cols = kvw // TP
    s = lax.axis_index("seq")
    t = lax.axis_index("tp")
    z = s // PLANE
    p = s % PLANE
    x = p // CORES
    c = p % CORES
    tm, tq, t2 = (t + TP - 1) % TP, (t + 1) % TP, (t + 2) % TP
    xm, xq, x2 = (x + XN - 1) % XN, (x + 1) % XN, (x + 2) % XN
    pm, pq, p2 = xm * CORES + c, xq * CORES + c, x2 * CORES + c
    po = x * CORES + 1 - c
    zq = (z + 1) % zn
    plane0 = z * PLANE
    other = (plane0 + po, t)
    xplus = (plane0 + pq, t)
    xminus = (plane0 + pm, t)
    zplus = (zq * PLANE + p, t)

    def remote(src, dst, ss, rs, dev):
        return pltpu.make_async_remote_copy(
            src_ref=src, dst_ref=dst, send_sem=ss, recv_sem=rs, device_id=dev, device_id_type=MESH
        )

    krows = wkv.shape[0]
    orows = wo.shape[0]
    cp_x = pltpu.make_async_copy(tokens_h, tokens, loc.at[2])
    cp_kv = pltpu.make_async_copy(wkv, wkvb.at[pl.ds(t * krows, krows), :], loc.at[0])
    cp_q = pltpu.make_async_copy(wq_h, wq, loc.at[3])
    cp_o = pltpu.make_async_copy(wo, wob.at[pl.ds(t * orows, orows), :], loc.at[1])

    barrier = pltpu.get_barrier_semaphore()
    for i in range(1, TP):
        pl.semaphore_signal(barrier, inc=1, device_id=(s, (t + i) % TP), device_id_type=MESH)
    for i in range(1, PLANE):
        pl.semaphore_signal(
            barrier, inc=1, device_id=(plane0 + (p + i) % PLANE, t), device_id_type=MESH
        )

    def greet(i, carry):
        pl.semaphore_signal(
            barrier, inc=1, device_id=(((z + i) % zn) * PLANE + p, t), device_id_type=MESH
        )
        return carry

    lax.fori_loop(1, zn, greet, 0)
    cp_x.start()
    cp_kv.start()
    cp_q.start()
    cp_o.start()
    pl.semaphore_wait(barrier, (TP - 1) + (PLANE - 1) + (zn - 1))

    def piece(w, ti, ci, part, parts):
        buf, n = (wkvb, krows) if w == 0 else (wob, orows)
        h = n // 2
        m = h // parts
        start = pl.multiple_of(ti * n + ci * h + part * m, 16)
        return buf.at[pl.ds(start, m), :]

    def wcopy(w, k, ti, part, parts, dev, r):
        ref = piece(w, ti, c, part, parts)
        src = ref
        if k < 2:
            n = (krows if w == 0 else orows) // 2
            src = (wkv if w == 0 else wo).at[pl.ds(pl.multiple_of(c * n, 16), n), :]
        return remote(src, ref, wss.at[w, k], wrs.at[w, r], dev)

    def wwait(w, r, ti, ci, part, parts):
        ref = piece(w, ti, ci, part, parts)
        remote(ref, ref, wss.at[w, r], wrs.at[w, r], other).wait_recv()

    def wsend(w, k):
        ti, part, parts, dev = (
            (t, 0, 1, (s, tq)),
            (t, 0, 1, (s, tm)),
            (tm, 0, 2, (s, tq)),
            (tq, 1, 2, (s, tm)),
            (tm, 0, 1, other),
            (tq, 0, 1, other),
            (t2, 0, 1, other),
        )[k]
        return wcopy(w, k, ti, part, parts, dev, k)

    def wfirst(w):
        wsend(w, 0).start()
        wsend(w, 1).start()

    def wrelay(w):
        wwait(w, 0, tm, c, 0, 1)
        wsend(w, 2).start()
        wsend(w, 4).start()
        wwait(w, 1, tq, c, 0, 1)
        wsend(w, 3).start()
        wsend(w, 5).start()

    def wlast(w):
        wwait(w, 2, t2, c, 0, 2)
        wwait(w, 3, t2, c, 1, 2)
        wsend(w, 6).start()

    def wdone(w):
        wwait(w, 4, tm, 1 - c, 0, 1)
        wwait(w, 5, tq, 1 - c, 0, 1)
        wwait(w, 6, t2, 1 - c, 0, 1)

    wfirst(0)
    cp_x.wait()

    step = 64

    def norm_rows(i, carry):
        r = pl.ds(pl.multiple_of(i * step, step), step)
        v = tokens[r, :].astype(F32)
        ms = jnp.mean(v * v, axis=1, keepdims=True)
        normed[r, :] = (v * lax.rsqrt(ms + EPS) * ngain[...]).astype(BF16)
        return carry

    lax.fori_loop(0, rows // step, norm_rows, 0)

    lens_f = lens[...].astype(F32)
    e0 = iota((nseg, nseg), 0)
    e1 = iota((nseg, nseg), 1)
    lens_b = jnp.broadcast_to(lens_f, (nseg, nseg))
    ends_col = jnp.sum(jnp.where(e1 <= e0, lens_b, 0.0), axis=1, keepdims=True)
    lens_col = jnp.sum(jnp.where(e1 == e0, lens_b, 0.0), axis=1, keepdims=True)
    starts_col = ends_col - lens_col
    f0 = iota((nseg, 128), 0)
    f1 = iota((nseg, 128), 1)
    ends_row = jnp.sum(jnp.where(f0 <= f1, lens_col, 0.0), axis=0, keepdims=True)
    starts_row = jnp.sum(jnp.where(f0 < f1, lens_col, 0.0), axis=0, keepdims=True)
    q_idx = (iota((1, rows), 1) + s * rows).astype(F32)
    inside = (starts_col <= q_idx) & (q_idx < ends_col)
    onehot_q = jnp.where(inside, 1.0, 0.0)
    first = jnp.sum(jnp.where(inside, starts_col, 0.0), axis=0, keepdims=True)
    angle = (q_idx - first) * freq[...]
    cosine = jnp.cos(angle)
    sine = jnp.sin(angle)
    g0 = iota((hd, hd), 0)
    g1 = iota((hd, hd), 1)
    qg = jnp.sum(jnp.where(g0 == g1, qgain[...], 0.0), axis=1, keepdims=True)
    kg = jnp.sum(jnp.where(g0 == g1, kgain[...], 0.0), axis=1, keepdims=True)

    def norm_rotate(h, gain):
        ms = jnp.mean(h * h, axis=0, keepdims=True)
        h = h * lax.rsqrt(ms + EPS) * gain
        u, w = h[:half], h[half:]
        return jnp.concatenate([u * cosine - w * sine, w * cosine + u * sine], axis=0)

    cp_q.wait()
    qt = dot(wq[...], normed[...], 1, 1)
    head0 = (t * ql) // group

    def pick(j):
        return (t * ql + j) // group - head0

    tail = jnp.concatenate([onehot_q, jnp.zeros((128 - nseg, rows), F32)], axis=0).astype(BF16)
    for j in range(ql):
        rot = norm_rotate(qt[j * hd : (j + 1) * hd], qg)
        second = (pick(j) == 1).astype(F32)
        lanes = slice(j * rows, (j + 1) * rows)
        qext[0:hd, lanes] = (rot * (1.0 - second)).astype(BF16)
        qext[hd : 2 * hd, lanes] = (rot * second).astype(BF16)
        qext[2 * hd :, lanes] = tail

    wrelay(0)
    wlast(0)
    wfirst(1)
    cp_kv.wait()
    cp_o.wait()
    wdone(0)
    kvf = jnp.transpose(dot(normed[...], wkvb[...]))
    for j in range(kvh):
        kvt[j * hd : (j + 1) * hd, :] = norm_rotate(kvf[j * hd : (j + 1) * hd], kg).astype(BF16)
    kvt[keyw:kvw, :] = kvf[keyw:kvw].astype(BF16)
    kt = kvt[pl.ds(pl.multiple_of(head0 * hd, hd), 2 * hd), :]
    vt = kvt[pl.ds(pl.multiple_of(keyw + head0 * hd, hd), 2 * hd), :]
    kv[0, p, 0:rows, :] = jnp.transpose(kt.astype(F32)).astype(BF16)
    kv[0, p, rows : rows + 128, :] = vt[:, 0:128]
    kv[0, p, rows + 128 : rows + 256, :] = vt[:, 128:256]

    def mixed(q):
        return jnp.where(q < p, 0, BACK)

    def kcopy(k, d):
        def whole(q):
            return kv.at[d, q]

        if k == 0:
            return remote(whole(p), kv.at[d + 1, p], kss.at[d, 0], krs.at[d + 1, p], zplus)
        if k == 1:
            return remote(whole(p), whole(p), kss.at[d, 1], krs.at[d, p], xplus)
        if k == 2:
            return remote(whole(p), whole(p), kss.at[d, 2], krs.at[d, p], xminus)
        if k == 3:
            return remote(whole(p), whole(p), kss.at[d, 3], krs.at[d, p], other)
        if k == 4:
            ref = kv.at[d, pm, pl.ds(0, rows), :]
            return remote(ref, ref, kss.at[d, 4], krs.at[d, pm], xplus)
        if k == 5:
            ref = kv.at[d, pq, pl.ds(rows, rows), :]
            return remote(ref, ref, kss.at[d, 5], krs2.at[d], xminus)
        q = (pm, pq, p2)[k - 6]
        return remote(whole(q), whole(q), kss.at[d, k], krs.at[d, q], other)

    after = {1: x < XN - 1, 2: x == 0, 3: c == 0, 4: x < XN // 2}

    def mcopy(k):
        if k < 5:
            e = jnp.where(after[k], 0, BACK)
            dev = {1: xplus, 2: xminus, 3: other, 4: (plane0 + p2, t)}[k]
            ref = kv.at[e, p]
            return remote(ref, ref, kss.at[0, k], krs.at[e, p], dev)
        q = (pm, pq, p2)[k - 6]
        ref = kv.at[mixed(q), q]
        return remote(ref, ref, kss.at[0, k], krs.at[mixed(q), q], other)

    def msend(first_part):
        for k in (4, 1, 2, 3):

            @pl.when(after[k] if first_part else jnp.logical_not(after[k]))
            def _(k=k):
                mcopy(k).start()

    def kwait(d, q):
        ref = kv.at[d, q]
        remote(ref, ref, kss.at[0, 0], krs.at[d, q], other).wait_recv()

    def arrive(d):
        kwait(d, p)
        if d < BACK:
            kcopy(0, d).start()
            for k in (1, 2, 3):
                kcopy(k, d).start()
        else:
            msend(False)

    def sides(d):
        kwait(d, pm)
        kcopy(4, d).start()
        kcopy(6, d).start()
        kwait(d, pq)
        kcopy(5, d).start()
        kcopy(7, d).start()

    def across(d):
        ref = kv.at[d, p2, pl.ds(0, rows), :]
        remote(ref, ref, kss.at[d, 4], krs.at[d, p2], other).wait_recv()
        ref = kv.at[d, p2, pl.ds(rows, rows), :]
        remote(ref, ref, kss.at[d, 5], krs2.at[d], other).wait_recv()
        kcopy(8, d).start()

    def mates(d):
        for i in range(XN):
            q = i * CORES + 1 - c
            kwait(mixed(q) if d == BACK else d, q)

    def mpass():
        for k, q in ((6, pm), (7, pq), (8, p2)):
            kwait(mixed(q), q)
            mcopy(k).start()

    kcopy(0, 0).start()
    msend(True)

    scale = float(1.0 / hd**0.5 * np.log2(np.e))

    def seg_mask(base):
        k_idx = (iota((rows, 128), 0) + base).astype(F32)
        outside = (k_idx < starts_row) | (k_idx >= ends_row)
        return jnp.where(outside, -FAR, 0.0).astype(BF16)

    causal = iota((rows, rows), 0) <= iota((rows, rows), 1)
    own_ext = jnp.concatenate([kv[0, p, 0:rows, :], seg_mask(s * rows)], axis=1)
    for j in range(ql):
        lanes = slice(j * rows, (j + 1) * rows)
        sc = jnp.where(causal, dot(own_ext, qext[:, lanes]), -FAR)
        m = jnp.max(sc, axis=0, keepdims=True)
        w = jnp.exp2((sc - m) * scale)
        mrun[:, lanes] = m
        lrun[:, lanes] = jnp.sum(w, axis=0, keepdims=True)
        acc[:, lanes] = dot(vt, w.astype(BF16))
    arrive(1)

    cap = pack.shape[0] // (zn * PLANE)
    owner_row = place[0:1, :].astype(F32)
    slot_row = place[1:2, :].astype(F32)
    same = iota((rows, rows), 0) == iota((rows, rows), 1)
    owner_col = jnp.sum(jnp.where(same, owner_row, 0.0), axis=1, keepdims=True)
    earlier = iota((rows, rows), 0) < iota((rows, rows), 1)
    rank = jnp.sum(
        jnp.where(earlier & (owner_col == owner_row), 1.0, 0.0), axis=0, keepdims=True
    )
    to_row = owner_row * cap + rank
    sel = jnp.where(iota((pack.shape[0], rows), 0).astype(F32) == to_row, 1.0, 0.0).astype(BF16)
    mine = kvt[pl.ds(pl.multiple_of(t * cols, 16), cols), :]
    extra = jnp.where(iota((pack.shape[1] - cols, rows), 0) == 0, slot_row + 1.0, 0.0)
    feats = jnp.concatenate([mine, extra.astype(BF16)], axis=0)
    pack[...] = dot(sel, feats, 1, 1).astype(BF16)
    zrows = PLANE * cap
    prows = zn * cap

    def zcopy(i):
        zt = (z + i) % zn
        return remote(
            pack.at[pl.ds(pl.multiple_of(zt * zrows, zrows), zrows), :],
            mid.at[pl.ds(pl.multiple_of(z * zrows, zrows), zrows), :],
            css.at[i], crs.at[z], (zt * PLANE + p, t),
        )

    def zstart(i, carry):
        zcopy(i).start()
        return carry

    def zwait(i, carry):
        zs = (z + i) % zn
        ref = mid.at[pl.ds(pl.multiple_of(zs * zrows, zrows), zrows), :]
        remote(ref, ref, css.at[i], crs.at[zs], other).wait_recv()
        return carry

    def pcopy(i):
        q = (p + i) % PLANE
        return remote(
            midp.at[pl.ds(pl.multiple_of(q * prows, prows), prows), :],
            fin.at[pl.ds(pl.multiple_of(p * prows, prows), prows), :],
            dss.at[i], drs.at[p], (plane0 + q, t),
        )

    def zsome(g):
        lax.fori_loop(1 + g * zn // 3, min(zn, 1 + (g + 1) * zn // 3), zstart, 0)

    zsome(0)
    zown = pl.ds(pl.multiple_of(z * zrows, zrows), zrows)
    mid[zown, :] = pack[zown, :]

    def cache_second():
        lax.fori_loop(1, zn, zwait, 0)
        n = pack.shape[0]
        r0 = iota((n, n), 0)
        r1 = iota((n, n), 1)
        src = ((r0 % prows) // cap) * zrows + (r0 // prows) * cap + r0 % cap
        perm = jnp.where(r1 == src, 1.0, 0.0).astype(BF16)
        midp[...] = dot(perm, mid[...]).astype(BF16)
        for i in range(1, PLANE):
            pcopy(i).start()
        pown = pl.ds(pl.multiple_of(p * prows, prows), prows)
        fin[pown, :] = midp[pown, :]

    sides(1)
    arrive(2)
    zsome(1)
    across(1)

    sub = PLANE // 2
    halves = PLANE // sub

    def turn(i, carry):
        d = 1 + i // halves
        for e in range(1, BACK + 1):

            @pl.when(i == (e - 1) * halves)
            def _(e=e):
                mates(e)

        ks, ms, vs = [], [], []
        for b in range(sub):
            q = (i % halves) * sub + b
            dq = jnp.where((d == BACK) & (q < p), 0, d)
            ks.append(kv[dq, q, 0:rows, :])
            ms.append(seg_mask(((z - dq) * PLANE + q) * rows))
            vs.append(kv[dq, q, rows : rows + 128, :])
            vs.append(kv[dq, q, rows + 128 : rows + 256, :])
        ext = jnp.concatenate([jnp.concatenate(ks, axis=0), jnp.concatenate(ms, axis=0)], axis=1)
        sc = dot(ext, qext[...])
        m = mrun[...]
        mn = jnp.maximum(m, jnp.max(sc, axis=0, keepdims=True))
        w = jnp.exp2((sc - mn) * scale)
        al = jnp.exp2((m - mn) * scale)
        lrun[...] = lrun[...] * al + jnp.sum(w, axis=0, keepdims=True)
        acc[...] = acc[...] * al + dot(jnp.concatenate(vs, axis=1), w.astype(BF16))
        mrun[...] = mn

        @pl.when(i == 0)
        def _():
            sides(2)

        @pl.when(i == 1)
        def _():
            across(2)
            arrive(3)
            zsome(2)

        @pl.when(i == 2)
        def _():
            sides(3)
            wrelay(1)

        @pl.when(i == 3)
        def _():
            across(3)
            arrive(4)

        @pl.when(i == 5)
        def _():
            mpass()
            wlast(1)
            cache_second()

        return carry

    lax.fori_loop(0, BACK * halves, turn, 0)

    for j in range(ql):
        lanes = slice(j * rows, (j + 1) * rows)
        o = acc[pl.ds(pl.multiple_of(pick(j) * hd, hd), hd), lanes] / lrun[:, lanes]
        att[:, j * hd : (j + 1) * hd] = jnp.transpose(o).astype(BF16)
    orow = rows // TP

    def acopy(i):
        ti = (t + i) % TP
        return remote(
            att.at[pl.ds(pl.multiple_of(ti * orow, orow), orow), :],
            attr.at[t], ess.at[i], ers.at[t], (s, ti),
        )

    for i in range(1, TP):
        acopy(i).start()
    attr[t] = att[pl.ds(pl.multiple_of(t * orow, orow), orow), :]

    for i in range(1, PLANE):
        q = (p + i) % PLANE
        ref = fin.at[pl.ds(pl.multiple_of(q * prows, prows), prows), :]
        remote(ref, ref, dss.at[i], drs.at[q], other).wait_recv()
    got = fin[...]
    slot_col = got[:, cols : cols + 1].astype(F32)
    n = pack.shape[0]
    put = jnp.where(slot_col == (iota((n, rows), 1) + 1).astype(F32), 1.0, 0.0).astype(BF16)
    cache[...] = dot(got, put, 0, 0)[0:cols, :].astype(BF16)

    wdone(1)
    for i in range(1, TP):
        ti = (t + i) % TP
        remote(attr.at[ti], attr.at[ti], ess.at[i], ers.at[ti], other).wait_recv()
    for ti in range(TP):
        attf[:, ti * ql * hd : (ti + 1) * ql * hd] = attr[ti]
    resid = tokens[pl.ds(pl.multiple_of(t * orow, orow), orow), :].astype(F32)
    hidden[...] = (dot(attf[...], wob[...]) + resid).astype(BF16)

    for w in range(2):
        for k in range(7):
            wsend(w, k).wait_send()

    kcopy(0, 0).wait_send()
    for k in (1, 2, 3, 4, 6, 7, 8):
        mcopy(k).wait_send()

    def kdone(d, carry):
        for k in range(9):
            kcopy(k, d).wait_send()
        return carry

    lax.fori_loop(1, BACK, kdone, 0)

    def zdone(i, carry):
        zcopy(i).wait_send()
        return carry

    lax.fori_loop(1, zn, zdone, 0)
    for i in range(1, PLANE):
        pcopy(i).wait_send()
    for i in range(1, TP):
        acopy(i).wait_send()


def per_device(tokens, norm_gain, q_gain, k_gain, w_query, w_keyval, w_out, lengths, cache_place):
    rows, width = tokens.shape
    seqs = lax.axis_size("seq")
    zn = seqs // PLANE
    hd = q_gain.shape[0]
    kvw = w_keyval.shape[1]
    cols = kvw // TP
    ql = w_query.shape[1] // hd
    cap = CAPACITY
    freq = (BASE ** (-(np.arange(hd // 2, dtype=np.float64) * 2.0) / hd)).astype(np.float32)
    vm = pl.BlockSpec(memory_space=pltpu.VMEM)
    hbm = pl.BlockSpec(memory_space=pl.ANY)
    packed = (seqs * cap, 256)
    dma = pltpu.SemaphoreType.DMA
    hidden, cache = pl.pallas_call(
        functools.partial(kernel, zn),
        out_shape=(
            jax.ShapeDtypeStruct((rows // TP, width), BF16),
            jax.ShapeDtypeStruct((cols, rows), BF16),
        ),
        in_specs=[vm] * 6 + [hbm] * 4,
        out_specs=(vm, vm),
        scratch_shapes=[
            pltpu.VMEM((rows, width), BF16),
            pltpu.VMEM((ql * hd, width), BF16),
            pltpu.VMEM((w_keyval.shape[0] * TP, kvw), BF16),
            pltpu.VMEM((w_out.shape[0] * TP, width), BF16),
            pltpu.VMEM((rows, width), BF16),
            pltpu.VMEM((kvw, rows), BF16),
            pltpu.VMEM((256, ql * rows), BF16),
            pltpu.VMEM((BACK + 1, PLANE, 2 * rows, 128), BF16),
            pltpu.VMEM((1, ql * rows), F32),
            pltpu.VMEM((1, ql * rows), F32),
            pltpu.VMEM((2 * hd, ql * rows), F32),
            pltpu.VMEM((rows, ql * hd), BF16),
            pltpu.VMEM((TP, rows // TP, ql * hd), BF16),
            pltpu.VMEM((rows // TP, TP * ql * hd), BF16),
            pltpu.VMEM(packed, BF16),
            pltpu.VMEM(packed, BF16),
            pltpu.VMEM(packed, BF16),
            pltpu.VMEM(packed, BF16),
            dma((4,)),
            dma((2, 7)),
            dma((2, 7)),
            dma((BACK + 1, 9)),
            dma((BACK + 1, PLANE)),
            dma((BACK + 1,)),
            dma((zn,)),
            dma((zn,)),
            dma((PLANE,)),
            dma((PLANE,)),
            dma((TP,)),
            dma((TP,)),
        ],
        compiler_params=pltpu.CompilerParams(
            collective_id=0, has_side_effects=True, vmem_limit_bytes=56 << 20
        ),
        name="layer",
    )(
        norm_gain.reshape(1, width),
        q_gain.reshape(1, hd),
        k_gain.reshape(1, hd),
        jnp.asarray(freq.reshape(-1, 1)),
        lengths.reshape(1, -1),
        cache_place.T,
        tokens,
        w_query.T,
        w_keyval,
        w_out,
    )
    return hidden, cache.T


CAPACITY = 4


def solution(mesh):
    placed = (
        P("seq", None),
        P(),
        P(),
        P(),
        P(None, "tp"),
        P("tp", None),
        P("tp", None),
        P(),
        P("seq", None),
    )
    return jax.shard_map(
        per_device,
        mesh=mesh,
        in_specs=placed,
        out_specs=(P(("seq", "tp"), None), P("seq", "tp")),
        check_vma=False,
    )
```

```python
import functools
import numpy as np
import jax
import jax.numpy as jnp
from jax import lax
from jax.experimental import pallas as pl
from jax.experimental.pallas import tpu as pltpu
from jax.sharding import PartitionSpec as P

EPS = 1e-06
BASE = 10000.0
FAR = 16384.0
MESH = pl.DeviceIdType.MESH
F32 = jnp.float32
BF16 = jnp.bfloat16
CORES = 2
XN = 4
PLANE = XN * CORES
BACK = 4
TP = 4


def dot(a, b, ca=1, cb=0):
    return lax.dot_general(a, b, (((ca,), (cb,)), ((), ())), preferred_element_type=F32)


def iota(shape, axis):
    return lax.broadcasted_iota(jnp.int32, shape, axis)


def kernel(
    zn, ngain, qgain, kgain, freq, lens, place, tokens_h, wq_h, wkv, wo,
    hidden, cache,
    tokens, wq, wraw, wt, wa, wc, wob, normed, kvt, qext, kv, mrun, lrun, acc, att, attr, attf,
    pack, mid, midp, fin, loc, aks, akr, afs, afr, wss, wrs, kss, krs, krs2, zss, zrs, css, crs, dss, drs, ess, ers,
):
    rows, width = tokens.shape
    hd = qgain.shape[1]
    half = hd // 2
    nseg = lens.shape[1]
    ql = wq.shape[0] // hd
    kvw = wkv.shape[1]
    keyw = kvw // 2
    kvh = keyw // hd
    group = ql * TP // kvh
    cols = kvw // TP
    s = lax.axis_index("seq")
    t = lax.axis_index("tp")
    z = s // PLANE
    p = s % PLANE
    x = p // CORES
    c = p % CORES
    tm, tq, t2 = (t + TP - 1) % TP, (t + 1) % TP, (t + 2) % TP
    xm, xq, x2 = (x + XN - 1) % XN, (x + 1) % XN, (x + 2) % XN
    pm, pq, p2 = xm * CORES + c, xq * CORES + c, x2 * CORES + c
    po = x * CORES + 1 - c
    zq = (z + 1) % zn
    plane0 = z * PLANE
    other = (plane0 + po, t)
    xplus = (plane0 + pq, t)
    xminus = (plane0 + pm, t)
    zplus = (zq * PLANE + p, t)

    def remote(src, dst, ss, rs, dev):
        return pltpu.make_async_remote_copy(
            src_ref=src, dst_ref=dst, send_sem=ss, recv_sem=rs, device_id=dev, device_id_type=MESH
        )

    krows = wkv.shape[0]
    orows = wo.shape[0]
    cp_x = pltpu.make_async_copy(tokens_h, tokens, loc.at[2])
    cp_kv = pltpu.make_async_copy(wkv, wraw, loc.at[0])
    cp_q = pltpu.make_async_copy(wq_h, wq, loc.at[3])
    cp_o = pltpu.make_async_copy(wo, wob.at[pl.ds(t * orows, orows), :], loc.at[1])

    barrier = pltpu.get_barrier_semaphore()
    for i in range(1, TP):
        pl.semaphore_signal(barrier, inc=1, device_id=(s, (t + i) % TP), device_id_type=MESH)
    for i in range(1, PLANE):
        pl.semaphore_signal(
            barrier, inc=1, device_id=(plane0 + (p + i) % PLANE, t), device_id_type=MESH
        )

    def greet(i, carry):
        pl.semaphore_signal(
            barrier, inc=1, device_id=(((z + i) % zn) * PLANE + p, t), device_id_type=MESH
        )
        return carry

    lax.fori_loop(1, zn, greet, 0)
    cp_kv.start()
    cp_x.start()
    cp_q.start()
    cp_o.start()
    cp_kv.wait()
    wt[...] = jnp.transpose(wraw[...])
    pl.semaphore_wait(barrier, (TP - 1) + (PLANE - 1) + (zn - 1))

    kh = krows // 2
    two = 2 * hd

    def first_head(ti):
        return (ti * ql) // group

    def need(g, ti):
        if g == 2:
            row = jnp.where(ti < TP // 2, ti * two, keyw + (ti - TP // 2) * two)
        else:
            row = first_head(ti) * hd + g * keyw
        return pl.ds(pl.multiple_of(row, hd), 3 * hd if g == 2 else two)

    def lanes_of(ts, ci):
        return pl.ds(pl.multiple_of(ts * krows + ci * kh, 128), kh)

    def placed(g, ts, ci):
        if g == 2:
            return wc.at[:, lanes_of(ts, ci)]
        return wa.at[pl.ds(g * two, two), lanes_of(ts, ci)]

    def asend(g, i):
        ti = (t + i) % TP
        src = wt.at[need(g, ti), pl.ds(pl.multiple_of(c * kh, 128), kh)]
        return remote(src, placed(g, t, c), aks.at[g, i], akr.at[g, t], (s, ti))

    def await_(g, i):
        ts = (t + i) % TP
        ref = placed(g, ts, c)
        remote(ref, ref, aks.at[g, i], akr.at[g, ts], other).wait_recv()

    def apass(g, i):
        ref = placed(g, (t + i) % TP, c)
        return remote(ref, ref, afs.at[g, i], afr.at[g, (t + i) % TP], other)

    def apassed(g, i):
        ts = (t + i) % TP
        ref = placed(g, ts, 1 - c)
        remote(ref, ref, afs.at[g, i], afr.at[g, ts], other).wait_recv()

    for i in (1, 3, 2):
        asend(0, i).start()
        asend(1, i).start()
    whole_own = pl.ds(pl.multiple_of(t * krows, 128), krows)
    wa[0:two, whole_own] = wt[need(0, t), :]
    wa[two : 2 * two, whole_own] = wt[need(1, t), :]
    wc[:, whole_own] = wt[need(2, t), :]

    def piece(w, ti, ci, part, parts):
        h = orows // 2
        m = h // parts
        start = pl.multiple_of(ti * orows + ci * h + part * m, 16)
        return wob.at[pl.ds(start, m), :]

    def wcopy(w, k, ti, part, parts, dev, r):
        ref = piece(w, ti, c, part, parts)
        src = ref
        if k < 2:
            n = orows // 2
            src = wo.at[pl.ds(pl.multiple_of(c * n, 16), n), :]
        return remote(src, ref, wss.at[w, k], wrs.at[w, r], dev)

    def wwait(w, r, ti, ci, part, parts):
        ref = piece(w, ti, ci, part, parts)
        remote(ref, ref, wss.at[w, r], wrs.at[w, r], other).wait_recv()

    def wsend(w, k):
        ti, part, parts, dev = (
            (t, 0, 1, (s, tq)),
            (t, 0, 1, (s, tm)),
            (tm, 0, 2, (s, tq)),
            (tq, 1, 2, (s, tm)),
            (tm, 0, 1, other),
            (tq, 0, 1, other),
            (t2, 0, 1, other),
        )[k]
        return wcopy(w, k, ti, part, parts, dev, k)

    def wfirst(w):
        wsend(w, 0).start()
        wsend(w, 1).start()

    def wrelay(w):
        wwait(w, 0, tm, c, 0, 1)
        wsend(w, 2).start()
        wsend(w, 4).start()
        wwait(w, 1, tq, c, 0, 1)
        wsend(w, 3).start()
        wsend(w, 5).start()

    def wlast(w):
        wwait(w, 2, t2, c, 0, 2)
        wwait(w, 3, t2, c, 1, 2)
        wsend(w, 6).start()

    def wdone(w):
        wwait(w, 4, tm, 1 - c, 0, 1)
        wwait(w, 5, tq, 1 - c, 0, 1)
        wwait(w, 6, t2, 1 - c, 0, 1)

    cp_x.wait()

    step = 64

    def norm_rows(i, carry):
        r = pl.ds(pl.multiple_of(i * step, step), step)
        v = tokens[r, :].astype(F32)
        ms = jnp.mean(v * v, axis=1, keepdims=True)
        normed[r, :] = (v * lax.rsqrt(ms + EPS) * ngain[...]).astype(BF16)
        return carry

    lax.fori_loop(0, rows // step, norm_rows, 0)

    lens_f = lens[...].astype(F32)
    e0 = iota((nseg, nseg), 0)
    e1 = iota((nseg, nseg), 1)
    lens_b = jnp.broadcast_to(lens_f, (nseg, nseg))
    ends_col = jnp.sum(jnp.where(e1 <= e0, lens_b, 0.0), axis=1, keepdims=True)
    lens_col = jnp.sum(jnp.where(e1 == e0, lens_b, 0.0), axis=1, keepdims=True)
    starts_col = ends_col - lens_col
    f0 = iota((nseg, 128), 0)
    f1 = iota((nseg, 128), 1)
    ends_row = jnp.sum(jnp.where(f0 <= f1, lens_col, 0.0), axis=0, keepdims=True)
    starts_row = jnp.sum(jnp.where(f0 < f1, lens_col, 0.0), axis=0, keepdims=True)
    q_idx = (iota((1, rows), 1) + s * rows).astype(F32)
    inside = (starts_col <= q_idx) & (q_idx < ends_col)
    onehot_q = jnp.where(inside, 1.0, 0.0)
    first = jnp.sum(jnp.where(inside, starts_col, 0.0), axis=0, keepdims=True)
    angle = (q_idx - first) * freq[...]
    cosine = jnp.cos(angle)
    sine = jnp.sin(angle)
    g0 = iota((hd, hd), 0)
    g1 = iota((hd, hd), 1)
    qg = jnp.sum(jnp.where(g0 == g1, qgain[...], 0.0), axis=1, keepdims=True)
    kg = jnp.sum(jnp.where(g0 == g1, kgain[...], 0.0), axis=1, keepdims=True)

    def norm_rotate(h, gain):
        ms = jnp.mean(h * h, axis=0, keepdims=True)
        h = h * lax.rsqrt(ms + EPS) * gain
        u, w = h[:half], h[half:]
        return jnp.concatenate([u * cosine - w * sine, w * cosine + u * sine], axis=0)

    cp_q.wait()
    qt = dot(wq[...], normed[...], 1, 1)
    head0 = (t * ql) // group

    def pick(j):
        return (t * ql + j) // group - head0

    tail = jnp.concatenate([onehot_q, jnp.zeros((128 - nseg, rows), F32)], axis=0).astype(BF16)
    for j in range(ql):
        rot = norm_rotate(qt[j * hd : (j + 1) * hd], qg)
        second = (pick(j) == 1).astype(F32)
        lanes = slice(j * rows, (j + 1) * rows)
        qext[0:hd, lanes] = (rot * (1.0 - second)).astype(BF16)
        qext[hd : 2 * hd, lanes] = (rot * second).astype(BF16)
        qext[2 * hd :, lanes] = tail

    for i in (1, 3, 2):
        for g in (0, 1):
            await_(g, i)
            apass(g, i).start()
    for i in (1, 3, 2):
        asend(2, i).start()
    cp_o.wait()
    wfirst(0)
    for i in (1, 3, 2):
        for g in (0, 1):
            apassed(g, i)
    kvf = dot(wa[...], normed[...], 1, 1)
    kt = jnp.concatenate(
        [norm_rotate(kvf[0:hd], kg), norm_rotate(kvf[hd:two], kg)], axis=0
    ).astype(BF16)
    vt = kvf[two : 2 * two].astype(BF16)
    kv[0, p, 0:rows, :] = jnp.transpose(kt.astype(F32)).astype(BF16)
    kv[0, p, rows : rows + 128, :] = vt[:, 0:128]
    kv[0, p, rows + 128 : rows + 256, :] = vt[:, 128:256]

    def mixed(q):
        return jnp.where(q < p, 0, BACK)

    def kcopy(k, d):
        def whole(q):
            return kv.at[d, q]

        if k == 1:
            return remote(whole(p), whole(p), kss.at[d, 1], krs.at[d, p], xplus)
        if k == 2:
            return remote(whole(p), whole(p), kss.at[d, 2], krs.at[d, p], xminus)
        if k == 3:
            return remote(whole(p), whole(p), kss.at[d, 3], krs.at[d, p], other)
        if k == 4:
            ref = kv.at[d, pm, pl.ds(0, rows), :]
            return remote(ref, ref, kss.at[d, 4], krs.at[d, pm], xplus)
        if k == 5:
            ref = kv.at[d, pq, pl.ds(rows, rows), :]
            return remote(ref, ref, kss.at[d, 5], krs2.at[d], xminus)
        q = (pm, pq, p2)[k - 6]
        return remote(whole(q), whole(q), kss.at[d, k], krs.at[d, q], other)

    after = {1: x < XN - 1, 2: x == 0, 3: c == 0, 4: x < XN // 2}

    def mcopy(k):
        if k < 5:
            e = jnp.where(after[k], 0, BACK)
            dev = {1: xplus, 2: xminus, 3: other, 4: (plane0 + p2, t)}[k]
            ref = kv.at[e, p]
            return remote(ref, ref, kss.at[0, k], krs.at[e, p], dev)
        q = (pm, pq, p2)[k - 6]
        ref = kv.at[mixed(q), q]
        return remote(ref, ref, kss.at[0, k], krs.at[mixed(q), q], other)

    def msend(first_part):
        for k in (4, 1, 2, 3):

            @pl.when(after[k] if first_part else jnp.logical_not(after[k]))
            def _(k=k):
                mcopy(k).start()

    def kwait(d, q):
        ref = kv.at[d, q]
        remote(ref, ref, kss.at[0, 1], krs.at[d, q], other).wait_recv()

    def hop(d, h):
        part = pl.ds(h * rows, rows)
        return remote(
            kv.at[d, p, part, :], kv.at[d + 1, p, part, :], zss.at[d, h], zrs.at[d + 1, h], zplus
        )

    def arrive(d):
        for h in range(2):
            ref = kv.at[d, p, pl.ds(h * rows, rows), :]
            remote(ref, ref, zss.at[0, h], zrs.at[d, h], other).wait_recv()
            if d < BACK:
                hop(d, h).start()
        if d < BACK:
            for k in (1, 2, 3):
                kcopy(k, d).start()
        else:
            msend(False)

    def sides(d):
        kwait(d, pm)
        kcopy(4, d).start()
        kcopy(6, d).start()
        kwait(d, pq)
        kcopy(5, d).start()
        kcopy(7, d).start()

    def across(d):
        ref = kv.at[d, p2, pl.ds(0, rows), :]
        remote(ref, ref, kss.at[d, 4], krs.at[d, p2], other).wait_recv()
        ref = kv.at[d, p2, pl.ds(rows, rows), :]
        remote(ref, ref, kss.at[d, 5], krs2.at[d], other).wait_recv()
        kcopy(8, d).start()

    def mates(d, xs):
        for xi in xs:
            q = xi * CORES + 1 - c
            kwait(mixed(q) if d == BACK else d, q)

    def mpass():
        for k, q in ((6, pm), (7, pq), (8, p2)):
            kwait(mixed(q), q)
            mcopy(k).start()

    hop(0, 0).start()
    hop(0, 1).start()
    msend(True)

    scale = float(1.0 / hd**0.5 * np.log2(np.e))

    def seg_mask(base):
        k_idx = (iota((rows, 128), 0) + base).astype(F32)
        outside = (k_idx < starts_row) | (k_idx >= ends_row)
        return jnp.where(outside, -FAR, 0.0).astype(BF16)

    causal = iota((rows, rows), 0) <= iota((rows, rows), 1)
    own_ext = jnp.concatenate([kv[0, p, 0:rows, :], seg_mask(s * rows)], axis=1)
    for j in range(ql):
        lanes = slice(j * rows, (j + 1) * rows)
        sc = jnp.where(causal, dot(own_ext, qext[:, lanes]), -FAR)
        m = jnp.max(sc, axis=0, keepdims=True)
        w = jnp.exp2((sc - m) * scale)
        mrun[:, lanes] = m
        lrun[:, lanes] = jnp.sum(w, axis=0, keepdims=True)
        acc[:, lanes] = dot(vt, w.astype(BF16))
    arrive(1)
    for i in (1, 3, 2):
        await_(2, i)
        apass(2, i).start()
    arrive(2)
    for i in (1, 3, 2):
        apassed(2, i)
    kvc = dot(wc[...], normed[...], 1, 1)
    for j in range(3):
        plain = kvc[j * hd : (j + 1) * hd]
        turned = jnp.where(t < TP // 2, norm_rotate(plain, kg), plain)
        kvt[j * hd : (j + 1) * hd, :] = turned.astype(BF16)

    cap = pack.shape[0] // (zn * PLANE)
    owner_row = place[0:1, :].astype(F32)
    slot_row = place[1:2, :].astype(F32)
    same = iota((rows, rows), 0) == iota((rows, rows), 1)
    owner_col = jnp.sum(jnp.where(same, owner_row, 0.0), axis=1, keepdims=True)
    earlier = iota((rows, rows), 0) < iota((rows, rows), 1)
    rank = jnp.sum(
        jnp.where(earlier & (owner_col == owner_row), 1.0, 0.0), axis=0, keepdims=True
    )
    to_row = owner_row * cap + rank
    sel = jnp.where(iota((pack.shape[0], rows), 0).astype(F32) == to_row, 1.0, 0.0).astype(BF16)
    skip = cols - two
    mine = kvt[pl.ds(pl.multiple_of((t % 2) * skip, 16), cols), :]
    extra = jnp.where(iota((pack.shape[1] - cols, rows), 0) == 0, slot_row + 1.0, 0.0)
    feats = jnp.concatenate([mine, extra.astype(BF16)], axis=0)
    pack[...] = dot(sel, feats, 1, 1).astype(BF16)
    zrows = PLANE * cap
    prows = zn * cap

    def zcopy(i):
        zt = (z + i) % zn
        return remote(
            pack.at[pl.ds(pl.multiple_of(zt * zrows, zrows), zrows), :],
            mid.at[pl.ds(pl.multiple_of(z * zrows, zrows), zrows), :],
            css.at[i], crs.at[z], (zt * PLANE + p, t),
        )

    def zstart(i, carry):
        zcopy(i).start()
        return carry

    def zwait(i, carry):
        zs = (z + i) % zn
        ref = mid.at[pl.ds(pl.multiple_of(zs * zrows, zrows), zrows), :]
        remote(ref, ref, css.at[i], crs.at[zs], other).wait_recv()
        return carry

    def pcopy(i):
        q = (p + i) % PLANE
        return remote(
            midp.at[pl.ds(pl.multiple_of(q * prows, prows), prows), :],
            fin.at[pl.ds(pl.multiple_of(p * prows, prows), prows), :],
            dss.at[i], drs.at[p], (plane0 + q, t),
        )

    lax.fori_loop(zn // 2 + 1, zn, zstart, 0)
    zown = pl.ds(pl.multiple_of(z * zrows, zrows), zrows)
    mid[zown, :] = pack[zown, :]

    def cache_second():
        lax.fori_loop(1, zn, zwait, 0)
        n = pack.shape[0]
        r0 = iota((n, n), 0)
        r1 = iota((n, n), 1)
        src = ((r0 % prows) // cap) * zrows + (r0 // prows) * cap + r0 % cap
        perm = jnp.where(r1 == src, 1.0, 0.0).astype(BF16)
        midp[...] = dot(perm, mid[...]).astype(BF16)
        for i in range(1, PLANE):
            pcopy(i).start()
        pown = pl.ds(pl.multiple_of(p * prows, prows), prows)
        fin[pown, :] = midp[pown, :]

    sides(1)
    arrive(3)

    sub = PLANE // 2
    halves = PLANE // sub

    def turn(i, carry):
        d = 1 + i // halves
        for e in range(1, BACK + 1):

            @pl.when(i == (e - 1) * halves)
            def _(e=e):
                mates(e, (x, xq))

            @pl.when(i == (e - 1) * halves + 1)
            def _(e=e):
                mates(e, (xm, x2))

        ks, ms, vs = [], [], []
        for b in range(sub):
            turned = b // CORES + (i % halves) * (XN // 2)
            q = ((x + turned) % XN) * CORES + b % CORES
            dq = jnp.where((d == BACK) & (q < p), 0, d)
            ks.append(kv[dq, q, 0:rows, :])
            ms.append(seg_mask(((z - dq) * PLANE + q) * rows))
            vs.append(kv[dq, q, rows : rows + 128, :])
            vs.append(kv[dq, q, rows + 128 : rows + 256, :])
        ext = jnp.concatenate([jnp.concatenate(ks, axis=0), jnp.concatenate(ms, axis=0)], axis=1)
        sc = dot(ext, qext[...])
        m = mrun[...]
        mn = jnp.maximum(m, jnp.max(sc, axis=0, keepdims=True))
        w = jnp.exp2((sc - mn) * scale)
        al = jnp.exp2((m - mn) * scale)
        lrun[...] = lrun[...] * al + jnp.sum(w, axis=0, keepdims=True)
        acc[...] = acc[...] * al + dot(jnp.concatenate(vs, axis=1), w.astype(BF16))
        mrun[...] = mn

        @pl.when(i == 0)
        def _():
            across(1)
            sides(2)
            arrive(4)
            lax.fori_loop(1, zn // 2 + 1, zstart, 0)

        @pl.when(i == 1)
        def _():
            across(2)
            sides(3)

        @pl.when(i == 2)
        def _():
            wrelay(0)

        @pl.when(i == 3)
        def _():
            across(3)

        @pl.when(i == 4)
        def _():
            mpass()

        @pl.when(i == 5)
        def _():
            wlast(0)
            cache_second()

        return carry

    lax.fori_loop(0, BACK * halves, turn, 0)

    for j in range(ql):
        lanes = slice(j * rows, (j + 1) * rows)
        o = acc[pl.ds(pl.multiple_of(pick(j) * hd, hd), hd), lanes] / lrun[:, lanes]
        att[:, j * hd : (j + 1) * hd] = jnp.transpose(o).astype(BF16)
    orow = rows // TP

    def acopy(i):
        ti = (t + i) % TP
        return remote(
            att.at[pl.ds(pl.multiple_of(ti * orow, orow), orow), :],
            attr.at[t], ess.at[i], ers.at[t], (s, ti),
        )

    for i in range(1, TP):
        acopy(i).start()
    attr[t] = att[pl.ds(pl.multiple_of(t * orow, orow), orow), :]

    for i in range(1, PLANE):
        q = (p + i) % PLANE
        ref = fin.at[pl.ds(pl.multiple_of(q * prows, prows), prows), :]
        remote(ref, ref, dss.at[i], drs.at[q], other).wait_recv()
    got = fin[...]
    slot_col = got[:, cols : cols + 1].astype(F32)
    n = pack.shape[0]
    put = jnp.where(slot_col == (iota((n, rows), 1) + 1).astype(F32), 1.0, 0.0).astype(BF16)
    cache[...] = dot(got, put, 0, 0)[0:cols, :].astype(BF16)

    wdone(0)
    for i in range(1, TP):
        ti = (t + i) % TP
        remote(attr.at[ti], attr.at[ti], ess.at[i], ers.at[ti], other).wait_recv()
    for ti in range(TP):
        attf[:, ti * ql * hd : (ti + 1) * ql * hd] = attr[ti]
    resid = tokens[pl.ds(pl.multiple_of(t * orow, orow), orow), :].astype(F32)
    hidden[...] = (dot(attf[...], wob[...]) + resid).astype(BF16)

    for k in range(7):
        wsend(0, k).wait_send()
    for g in range(3):
        for i in range(1, TP):
            asend(g, i).wait_send()
            apass(g, i).wait_send()

    for k in (1, 2, 3, 4, 6, 7, 8):
        mcopy(k).wait_send()

    def kdone(d, carry):
        for k in range(1, 9):
            kcopy(k, d).wait_send()
        return carry

    lax.fori_loop(1, BACK, kdone, 0)

    def hdone(d, carry):
        hop(d, 0).wait_send()
        hop(d, 1).wait_send()
        return carry

    lax.fori_loop(0, BACK, hdone, 0)

    def zdone(i, carry):
        zcopy(i).wait_send()
        return carry

    lax.fori_loop(1, zn, zdone, 0)
    for i in range(1, PLANE):
        pcopy(i).wait_send()
    for i in range(1, TP):
        acopy(i).wait_send()


def per_device(tokens, norm_gain, q_gain, k_gain, w_query, w_keyval, w_out, lengths, cache_place):
    rows, width = tokens.shape
    seqs = lax.axis_size("seq")
    zn = seqs // PLANE
    hd = q_gain.shape[0]
    kvw = w_keyval.shape[1]
    cols = kvw // TP
    ql = w_query.shape[1] // hd
    cap = CAPACITY
    freq = (BASE ** (-(np.arange(hd // 2, dtype=np.float64) * 2.0) / hd)).astype(np.float32)
    vm = pl.BlockSpec(memory_space=pltpu.VMEM)
    hbm = pl.BlockSpec(memory_space=pl.ANY)
    packed = (seqs * cap, 256)
    dma = pltpu.SemaphoreType.DMA
    hidden, cache = pl.pallas_call(
        functools.partial(kernel, zn),
        out_shape=(
            jax.ShapeDtypeStruct((rows // TP, width), BF16),
            jax.ShapeDtypeStruct((cols, rows), BF16),
        ),
        in_specs=[vm] * 6 + [hbm] * 4,
        out_specs=(vm, vm),
        scratch_shapes=[
            pltpu.VMEM((rows, width), BF16),
            pltpu.VMEM((ql * hd, width), BF16),
            pltpu.VMEM((w_keyval.shape[0], kvw), BF16),
            pltpu.VMEM((kvw, w_keyval.shape[0]), BF16),
            pltpu.VMEM((4 * hd, width), BF16),
            pltpu.VMEM((3 * hd, width), BF16),
            pltpu.VMEM((w_out.shape[0] * TP, width), BF16),
            pltpu.VMEM((rows, width), BF16),
            pltpu.VMEM((3 * hd, rows), BF16),
            pltpu.VMEM((256, ql * rows), BF16),
            pltpu.VMEM((BACK + 1, PLANE, 2 * rows, 128), BF16),
            pltpu.VMEM((1, ql * rows), F32),
            pltpu.VMEM((1, ql * rows), F32),
            pltpu.VMEM((2 * hd, ql * rows), F32),
            pltpu.VMEM((rows, ql * hd), BF16),
            pltpu.VMEM((TP, rows // TP, ql * hd), BF16),
            pltpu.VMEM((rows // TP, TP * ql * hd), BF16),
            pltpu.VMEM(packed, BF16),
            pltpu.VMEM(packed, BF16),
            pltpu.VMEM(packed, BF16),
            pltpu.VMEM(packed, BF16),
            dma((4,)),
            dma((3, TP)),
            dma((3, TP)),
            dma((3, TP)),
            dma((3, TP)),
            dma((1, 7)),
            dma((1, 7)),
            dma((BACK + 1, 9)),
            dma((BACK + 1, PLANE)),
            dma((BACK + 1,)),
            dma((BACK, 2)),
            dma((BACK + 1, 2)),
            dma((zn,)),
            dma((zn,)),
            dma((PLANE,)),
            dma((PLANE,)),
            dma((TP,)),
            dma((TP,)),
        ],
        compiler_params=pltpu.CompilerParams(
            collective_id=0, has_side_effects=True, vmem_limit_bytes=56 << 20
        ),
        name="layer",
    )(
        norm_gain.reshape(1, width),
        q_gain.reshape(1, hd),
        k_gain.reshape(1, hd),
        jnp.asarray(freq.reshape(-1, 1)),
        lengths.reshape(1, -1),
        cache_place.T,
        tokens,
        w_query.T,
        w_keyval,
        w_out,
    )
    return hidden, cache.T


CAPACITY = 4


def solution(mesh):
    placed = (
        P("seq", None),
        P(),
        P(),
        P(),
        P(None, "tp"),
        P("tp", None),
        P("tp", None),
        P(),
        P("seq", None),
    )
    return jax.shard_map(
        per_device,
        mesh=mesh,
        in_specs=placed,
        out_specs=(P(("seq", "tp"), None), P("seq", "tp")),
        check_vma=False,
    )
```

```python
import functools
import numpy as np
import jax
import jax.numpy as jnp
from jax import lax
from jax.experimental import pallas as pl
from jax.experimental.pallas import tpu as pltpu
from jax.sharding import PartitionSpec as P

EPS = 1e-06
BASE = 10000.0
FAR = 16384.0
MESH = pl.DeviceIdType.MESH
F32 = jnp.float32
BF16 = jnp.bfloat16
CORES = 2
XN = 4
PLANE = XN * CORES
BACK = 4
TP = 4


def dot(a, b, ca=1, cb=0):
    return lax.dot_general(a, b, (((ca,), (cb,)), ((), ())), preferred_element_type=F32)


def iota(shape, axis):
    return lax.broadcasted_iota(jnp.int32, shape, axis)


def kernel(
    zn, ngain, qgain, kgain, freq, lens, place, tokens_h, wq_h, wkv, wo,
    hidden, cache,
    tokens, wq, wraw, wt, wa, wc, wob, normed, kvt, qext, kv, mrun, lrun, acc, att, attr, attf,
    pack, mid, midp, fin, loc, aks, akr, afs, afr, met, wss, wrs, kss, krs, krs2, zss, zrs, css, crs, dss, drs, ess, ers,
):
    rows, width = tokens.shape
    hd = qgain.shape[1]
    half = hd // 2
    nseg = lens.shape[1]
    ql = wq.shape[0] // hd
    kvw = wkv.shape[1]
    keyw = kvw // 2
    kvh = keyw // hd
    group = ql * TP // kvh
    cols = kvw // TP
    s = lax.axis_index("seq")
    t = lax.axis_index("tp")
    z = s // PLANE
    p = s % PLANE
    x = p // CORES
    c = p % CORES
    tm, tq, t2 = (t + TP - 1) % TP, (t + 1) % TP, (t + 2) % TP
    xm, xq, x2 = (x + XN - 1) % XN, (x + 1) % XN, (x + 2) % XN
    pm, pq, p2 = xm * CORES + c, xq * CORES + c, x2 * CORES + c
    po = x * CORES + 1 - c
    zq = (z + 1) % zn
    plane0 = z * PLANE
    other = (plane0 + po, t)
    xplus = (plane0 + pq, t)
    xminus = (plane0 + pm, t)
    zplus = (zq * PLANE + p, t)

    def remote(src, dst, ss, rs, dev):
        return pltpu.make_async_remote_copy(
            src_ref=src, dst_ref=dst, send_sem=ss, recv_sem=rs, device_id=dev, device_id_type=MESH
        )

    krows = wkv.shape[0]
    orows = wo.shape[0]
    cp_x = pltpu.make_async_copy(tokens_h, tokens, loc.at[2])
    cp_kv = pltpu.make_async_copy(wkv, wraw, loc.at[0])
    cp_q = pltpu.make_async_copy(wq_h, wq, loc.at[3])
    cp_o = pltpu.make_async_copy(wo, wob.at[pl.ds(t * orows, orows), :], loc.at[1])

    barrier = pltpu.get_barrier_semaphore()
    for i in range(1, TP):
        pl.semaphore_signal(barrier, inc=1, device_id=(s, (t + i) % TP), device_id_type=MESH)
    for i in range(1, PLANE):
        pl.semaphore_signal(
            barrier, inc=1, device_id=(plane0 + (p + i) % PLANE, t), device_id_type=MESH
        )

    for i in (1, zn - 1):
        pl.semaphore_signal(
            barrier, inc=1, device_id=(((z + i) % zn) * PLANE + p, t), device_id_type=MESH
        )

    def meet(r):
        for side, i in ((0, 1 << r), (1, zn - (1 << r))):
            pl.semaphore_signal(
                met.at[r, side], inc=1,
                device_id=(((z + i) % zn) * PLANE + p, t), device_id_type=MESH,
            )

    def known(r):
        for side in (0, 1):
            pl.semaphore_wait(met.at[r, side], 1)

    cp_kv.start()
    cp_x.start()
    cp_q.start()
    cp_o.start()
    cp_kv.wait()
    wt[...] = jnp.transpose(wraw[...])
    pl.semaphore_wait(barrier, (TP - 1) + (PLANE - 1) + 2)
    meet(0)

    kh = krows // 2
    two = 2 * hd

    def first_head(ti):
        return (ti * ql) // group

    def need(g, ti):
        if g == 2:
            row = jnp.where(ti < TP // 2, ti * two, keyw + (ti - TP // 2) * two)
        else:
            row = first_head(ti) * hd + g * keyw
        return pl.ds(pl.multiple_of(row, hd), 3 * hd if g == 2 else two)

    def lanes_of(ts, ci):
        return pl.ds(pl.multiple_of(ts * krows + ci * kh, 128), kh)

    def placed(g, ts, ci):
        if g == 2:
            return wc.at[:, lanes_of(ts, ci)]
        return wa.at[pl.ds(g * two, two), lanes_of(ts, ci)]

    def asend(g, i):
        ti = (t + i) % TP
        src = wt.at[need(g, ti), pl.ds(pl.multiple_of(c * kh, 128), kh)]
        return remote(src, placed(g, t, c), aks.at[g, i], akr.at[g, t], (s, ti))

    def await_(g, i):
        ts = (t + i) % TP
        ref = placed(g, ts, c)
        remote(ref, ref, aks.at[g, i], akr.at[g, ts], other).wait_recv()

    def apass(g, i):
        ref = placed(g, (t + i) % TP, c)
        return remote(ref, ref, afs.at[g, i], afr.at[g, (t + i) % TP], other)

    def apassed(g, i):
        ts = (t + i) % TP
        ref = placed(g, ts, 1 - c)
        remote(ref, ref, afs.at[g, i], afr.at[g, ts], other).wait_recv()

    for i in (1, 3, 2):
        asend(0, i).start()
        asend(1, i).start()
    whole_own = pl.ds(pl.multiple_of(t * krows, 128), krows)
    wa[0:two, whole_own] = wt[need(0, t), :]
    wa[two : 2 * two, whole_own] = wt[need(1, t), :]
    wc[:, whole_own] = wt[need(2, t), :]

    def piece(w, ti, ci, part, parts):
        h = orows // 2
        m = h // parts
        start = pl.multiple_of(ti * orows + ci * h + part * m, 16)
        return wob.at[pl.ds(start, m), :]

    def wcopy(w, k, ti, part, parts, dev, r):
        ref = piece(w, ti, c, part, parts)
        src = ref
        if k < 2:
            n = orows // 2
            src = wo.at[pl.ds(pl.multiple_of(c * n, 16), n), :]
        return remote(src, ref, wss.at[w, k], wrs.at[w, r], dev)

    def wwait(w, r, ti, ci, part, parts):
        ref = piece(w, ti, ci, part, parts)
        remote(ref, ref, wss.at[w, r], wrs.at[w, r], other).wait_recv()

    def wsend(w, k):
        ti, part, parts, dev = (
            (t, 0, 1, (s, tq)),
            (t, 0, 1, (s, tm)),
            (tm, 0, 2, (s, tq)),
            (tq, 1, 2, (s, tm)),
            (tm, 0, 1, other),
            (tq, 0, 1, other),
            (t2, 0, 1, other),
        )[k]
        return wcopy(w, k, ti, part, parts, dev, k)

    def wfirst(w):
        wsend(w, 0).start()
        wsend(w, 1).start()

    def wrelay(w):
        wwait(w, 0, tm, c, 0, 1)
        wsend(w, 2).start()
        wsend(w, 4).start()
        wwait(w, 1, tq, c, 0, 1)
        wsend(w, 3).start()
        wsend(w, 5).start()

    def wlast(w):
        wwait(w, 2, t2, c, 0, 2)
        wwait(w, 3, t2, c, 1, 2)
        wsend(w, 6).start()

    def wdone(w):
        wwait(w, 4, tm, 1 - c, 0, 1)
        wwait(w, 5, tq, 1 - c, 0, 1)
        wwait(w, 6, t2, 1 - c, 0, 1)

    cp_x.wait()

    step = 64

    def norm_rows(i, carry):
        r = pl.ds(pl.multiple_of(i * step, step), step)
        v = tokens[r, :].astype(F32)
        ms = jnp.mean(v * v, axis=1, keepdims=True)
        normed[r, :] = (v * lax.rsqrt(ms + EPS) * ngain[...]).astype(BF16)
        return carry

    lax.fori_loop(0, rows // step, norm_rows, 0)

    lens_f = lens[...].astype(F32)
    e0 = iota((nseg, nseg), 0)
    e1 = iota((nseg, nseg), 1)
    lens_b = jnp.broadcast_to(lens_f, (nseg, nseg))
    ends_col = jnp.sum(jnp.where(e1 <= e0, lens_b, 0.0), axis=1, keepdims=True)
    lens_col = jnp.sum(jnp.where(e1 == e0, lens_b, 0.0), axis=1, keepdims=True)
    starts_col = ends_col - lens_col
    f0 = iota((nseg, 128), 0)
    f1 = iota((nseg, 128), 1)
    ends_row = jnp.sum(jnp.where(f0 <= f1, lens_col, 0.0), axis=0, keepdims=True)
    starts_row = jnp.sum(jnp.where(f0 < f1, lens_col, 0.0), axis=0, keepdims=True)
    q_idx = (iota((1, rows), 1) + s * rows).astype(F32)
    inside = (starts_col <= q_idx) & (q_idx < ends_col)
    onehot_q = jnp.where(inside, 1.0, 0.0)
    first = jnp.sum(jnp.where(inside, starts_col, 0.0), axis=0, keepdims=True)
    angle = (q_idx - first) * freq[...]
    cosine = jnp.cos(angle)
    sine = jnp.sin(angle)
    g0 = iota((hd, hd), 0)
    g1 = iota((hd, hd), 1)
    qg = jnp.sum(jnp.where(g0 == g1, qgain[...], 0.0), axis=1, keepdims=True)
    kg = jnp.sum(jnp.where(g0 == g1, kgain[...], 0.0), axis=1, keepdims=True)

    def norm_rotate(h, gain):
        ms = jnp.mean(h * h, axis=0, keepdims=True)
        h = h * lax.rsqrt(ms + EPS) * gain
        u, w = h[:half], h[half:]
        return jnp.concatenate([u * cosine - w * sine, w * cosine + u * sine], axis=0)

    known(0)
    meet(1)
    cp_q.wait()
    qt = dot(wq[...], normed[...], 1, 1)
    head0 = (t * ql) // group

    def pick(j):
        return (t * ql + j) // group - head0

    tail = jnp.concatenate([onehot_q, jnp.zeros((128 - nseg, rows), F32)], axis=0).astype(BF16)
    for j in range(ql):
        rot = norm_rotate(qt[j * hd : (j + 1) * hd], qg)
        second = (pick(j) == 1).astype(F32)
        lanes = slice(j * rows, (j + 1) * rows)
        qext[0:hd, lanes] = (rot * (1.0 - second)).astype(BF16)
        qext[hd : 2 * hd, lanes] = (rot * second).astype(BF16)
        qext[2 * hd :, lanes] = tail

    for i in (1, 3, 2):
        for g in (0, 1):
            await_(g, i)
            apass(g, i).start()
    for i in (1, 3, 2):
        asend(2, i).start()
    cp_o.wait()
    wfirst(0)
    for i in (1, 3, 2):
        for g in (0, 1):
            apassed(g, i)
    known(1)
    meet(2)
    kvf = dot(wa[...], normed[...], 1, 1)
    kt = jnp.concatenate(
        [norm_rotate(kvf[0:hd], kg), norm_rotate(kvf[hd:two], kg)], axis=0
    ).astype(BF16)
    vt = kvf[two : 2 * two].astype(BF16)
    kv[0, p, 0:rows, :] = jnp.transpose(kt.astype(F32)).astype(BF16)
    kv[0, p, rows : rows + 128, :] = vt[:, 0:128]
    kv[0, p, rows + 128 : rows + 256, :] = vt[:, 128:256]

    def mixed(q):
        return jnp.where(q < p, 0, BACK)

    def kcopy(k, d):
        def whole(q):
            return kv.at[d, q]

        if k == 1:
            return remote(whole(p), whole(p), kss.at[d, 1], krs.at[d, p], xplus)
        if k == 2:
            return remote(whole(p), whole(p), kss.at[d, 2], krs.at[d, p], xminus)
        if k == 3:
            return remote(whole(p), whole(p), kss.at[d, 3], krs.at[d, p], other)
        if k == 4:
            ref = kv.at[d, pm, pl.ds(0, rows), :]
            return remote(ref, ref, kss.at[d, 4], krs.at[d, pm], xplus)
        if k == 5:
            ref = kv.at[d, pq, pl.ds(rows, rows), :]
            return remote(ref, ref, kss.at[d, 5], krs2.at[d], xminus)
        q = (pm, pq, p2)[k - 6]
        return remote(whole(q), whole(q), kss.at[d, k], krs.at[d, q], other)

    after = {1: x < XN - 1, 2: x == 0, 3: c == 0, 4: x < XN // 2}

    def mcopy(k):
        if k < 5:
            e = jnp.where(after[k], 0, BACK)
            dev = {1: xplus, 2: xminus, 3: other, 4: (plane0 + p2, t)}[k]
            ref = kv.at[e, p]
            return remote(ref, ref, kss.at[0, k], krs.at[e, p], dev)
        q = (pm, pq, p2)[k - 6]
        ref = kv.at[mixed(q), q]
        return remote(ref, ref, kss.at[0, k], krs.at[mixed(q), q], other)

    def msend(first_part):
        for k in (4, 1, 2, 3):

            @pl.when(after[k] if first_part else jnp.logical_not(after[k]))
            def _(k=k):
                mcopy(k).start()

    def kwait(d, q):
        ref = kv.at[d, q]
        remote(ref, ref, kss.at[0, 1], krs.at[d, q], other).wait_recv()

    def hop(d, h):
        part = pl.ds(h * rows, rows)
        return remote(
            kv.at[d, p, part, :], kv.at[d + 1, p, part, :], zss.at[d, h], zrs.at[d + 1, h], zplus
        )

    def arrive(d):
        for h in range(2):
            ref = kv.at[d, p, pl.ds(h * rows, rows), :]
            remote(ref, ref, zss.at[0, h], zrs.at[d, h], other).wait_recv()
            if d < BACK:
                hop(d, h).start()
        if d < BACK:
            for k in (1, 2, 3):
                kcopy(k, d).start()
        else:
            msend(False)

    def sides(d):
        kwait(d, pm)
        kcopy(4, d).start()
        kcopy(6, d).start()
        kwait(d, pq)
        kcopy(5, d).start()
        kcopy(7, d).start()

    def across(d):
        ref = kv.at[d, p2, pl.ds(0, rows), :]
        remote(ref, ref, kss.at[d, 4], krs.at[d, p2], other).wait_recv()
        ref = kv.at[d, p2, pl.ds(rows, rows), :]
        remote(ref, ref, kss.at[d, 5], krs2.at[d], other).wait_recv()
        kcopy(8, d).start()

    def mates(d, xs):
        for xi in xs:
            q = xi * CORES + 1 - c
            kwait(mixed(q) if d == BACK else d, q)

    def mpass():
        for k, q in ((6, pm), (7, pq), (8, p2)):
            kwait(mixed(q), q)
            mcopy(k).start()

    hop(0, 0).start()
    hop(0, 1).start()
    msend(True)

    scale = float(1.0 / hd**0.5 * np.log2(np.e))

    def seg_mask(base):
        k_idx = (iota((rows, 128), 0) + base).astype(F32)
        outside = (k_idx < starts_row) | (k_idx >= ends_row)
        return jnp.where(outside, -FAR, 0.0).astype(BF16)

    causal = iota((rows, rows), 0) <= iota((rows, rows), 1)
    own_ext = jnp.concatenate([kv[0, p, 0:rows, :], seg_mask(s * rows)], axis=1)
    for j in range(ql):
        lanes = slice(j * rows, (j + 1) * rows)
        sc = jnp.where(causal, dot(own_ext, qext[:, lanes]), -FAR)
        m = jnp.max(sc, axis=0, keepdims=True)
        w = jnp.exp2((sc - m) * scale)
        mrun[:, lanes] = m
        lrun[:, lanes] = jnp.sum(w, axis=0, keepdims=True)
        acc[:, lanes] = dot(vt, w.astype(BF16))
    arrive(1)
    for i in (1, 3, 2):
        await_(2, i)
        apass(2, i).start()
    arrive(2)
    for i in (1, 3, 2):
        apassed(2, i)
    kvc = dot(wc[...], normed[...], 1, 1)
    for j in range(3):
        plain = kvc[j * hd : (j + 1) * hd]
        turned = jnp.where(t < TP // 2, norm_rotate(plain, kg), plain)
        kvt[j * hd : (j + 1) * hd, :] = turned.astype(BF16)

    cap = pack.shape[0] // (zn * PLANE)
    owner_row = place[0:1, :].astype(F32)
    slot_row = place[1:2, :].astype(F32)
    same = iota((rows, rows), 0) == iota((rows, rows), 1)
    owner_col = jnp.sum(jnp.where(same, owner_row, 0.0), axis=1, keepdims=True)
    earlier = iota((rows, rows), 0) < iota((rows, rows), 1)
    rank = jnp.sum(
        jnp.where(earlier & (owner_col == owner_row), 1.0, 0.0), axis=0, keepdims=True
    )
    to_row = owner_row * cap + rank
    sel = jnp.where(iota((pack.shape[0], rows), 0).astype(F32) == to_row, 1.0, 0.0).astype(BF16)
    skip = cols - two
    mine = kvt[pl.ds(pl.multiple_of((t % 2) * skip, 16), cols), :]
    extra = jnp.where(iota((pack.shape[1] - cols, rows), 0) == 0, slot_row + 1.0, 0.0)
    feats = jnp.concatenate([mine, extra.astype(BF16)], axis=0)
    pack[...] = dot(sel, feats, 1, 1).astype(BF16)
    zrows = PLANE * cap
    prows = zn * cap

    def zcopy(i):
        zt = (z + i) % zn
        return remote(
            pack.at[pl.ds(pl.multiple_of(zt * zrows, zrows), zrows), :],
            mid.at[pl.ds(pl.multiple_of(z * zrows, zrows), zrows), :],
            css.at[i], crs.at[z], (zt * PLANE + p, t),
        )

    def zstart(i, carry):
        zcopy(i).start()
        return carry

    def zwait(i, carry):
        zs = (z + i) % zn
        ref = mid.at[pl.ds(pl.multiple_of(zs * zrows, zrows), zrows), :]
        remote(ref, ref, css.at[i], crs.at[zs], other).wait_recv()
        return carry

    def pcopy(i):
        q = (p + i) % PLANE
        return remote(
            midp.at[pl.ds(pl.multiple_of(q * prows, prows), prows), :],
            fin.at[pl.ds(pl.multiple_of(p * prows, prows), prows), :],
            dss.at[i], drs.at[p], (plane0 + q, t),
        )

    known(2)
    lax.fori_loop(zn // 2 + 1, zn, zstart, 0)
    zown = pl.ds(pl.multiple_of(z * zrows, zrows), zrows)
    mid[zown, :] = pack[zown, :]

    def cache_second():
        lax.fori_loop(1, zn, zwait, 0)
        n = pack.shape[0]
        r0 = iota((n, n), 0)
        r1 = iota((n, n), 1)
        src = ((r0 % prows) // cap) * zrows + (r0 // prows) * cap + r0 % cap
        perm = jnp.where(r1 == src, 1.0, 0.0).astype(BF16)
        midp[...] = dot(perm, mid[...]).astype(BF16)
        for i in range(1, PLANE):
            pcopy(i).start()
        pown = pl.ds(pl.multiple_of(p * prows, prows), prows)
        fin[pown, :] = midp[pown, :]

    sides(1)
    arrive(3)

    sub = PLANE // 2
    halves = PLANE // sub

    def turn(i, carry):
        d = 1 + i // halves
        for e in range(1, BACK + 1):

            @pl.when(i == (e - 1) * halves)
            def _(e=e):
                mates(e, (x, xq))

            @pl.when(i == (e - 1) * halves + 1)
            def _(e=e):
                mates(e, (xm, x2))

        ks, ms, vs = [], [], []
        for b in range(sub):
            turned = b // CORES + (i % halves) * (XN // 2)
            q = ((x + turned) % XN) * CORES + b % CORES
            dq = jnp.where((d == BACK) & (q < p), 0, d)
            ks.append(kv[dq, q, 0:rows, :])
            ms.append(seg_mask(((z - dq) * PLANE + q) * rows))
            vs.append(kv[dq, q, rows : rows + 128, :])
            vs.append(kv[dq, q, rows + 128 : rows + 256, :])
        ext = jnp.concatenate([jnp.concatenate(ks, axis=0), jnp.concatenate(ms, axis=0)], axis=1)
        sc = dot(ext, qext[...])
        m = mrun[...]
        mn = jnp.maximum(m, jnp.max(sc, axis=0, keepdims=True))
        w = jnp.exp2((sc - mn) * scale)
        al = jnp.exp2((m - mn) * scale)
        lrun[...] = lrun[...] * al + jnp.sum(w, axis=0, keepdims=True)
        acc[...] = acc[...] * al + dot(jnp.concatenate(vs, axis=1), w.astype(BF16))
        mrun[...] = mn

        @pl.when(i == 0)
        def _():
            across(1)
            sides(2)
            arrive(4)
            lax.fori_loop(1, zn // 2 + 1, zstart, 0)

        @pl.when(i == 1)
        def _():
            across(2)
            sides(3)

        @pl.when(i == 2)
        def _():
            wrelay(0)

        @pl.when(i == 3)
        def _():
            across(3)

        @pl.when(i == 4)
        def _():
            mpass()

        @pl.when(i == 5)
        def _():
            wlast(0)
            cache_second()

        return carry

    lax.fori_loop(0, BACK * halves, turn, 0)

    for j in range(ql):
        lanes = slice(j * rows, (j + 1) * rows)
        o = acc[pl.ds(pl.multiple_of(pick(j) * hd, hd), hd), lanes] / lrun[:, lanes]
        att[:, j * hd : (j + 1) * hd] = jnp.transpose(o).astype(BF16)
    orow = rows // TP

    def acopy(i):
        ti = (t + i) % TP
        return remote(
            att.at[pl.ds(pl.multiple_of(ti * orow, orow), orow), :],
            attr.at[t], ess.at[i], ers.at[t], (s, ti),
        )

    for i in range(1, TP):
        acopy(i).start()
    attr[t] = att[pl.ds(pl.multiple_of(t * orow, orow), orow), :]

    for k in range(7):
        wsend(0, k).wait_send()
    for g in range(3):
        for i in range(1, TP):
            asend(g, i).wait_send()
            apass(g, i).wait_send()

    for k in (1, 2, 3, 4, 6, 7, 8):
        mcopy(k).wait_send()

    def kdone(d, carry):
        for k in range(1, 9):
            kcopy(k, d).wait_send()
        return carry

    lax.fori_loop(1, BACK, kdone, 0)

    def hdone(d, carry):
        hop(d, 0).wait_send()
        hop(d, 1).wait_send()
        return carry

    lax.fori_loop(0, BACK, hdone, 0)

    def zdone(i, carry):
        zcopy(i).wait_send()
        return carry

    lax.fori_loop(1, zn, zdone, 0)
    wdone(0)
    for i in range(1, TP):
        ti = (t + i) % TP
        remote(attr.at[ti], attr.at[ti], ess.at[i], ers.at[ti], other).wait_recv()
    for ti in range(TP):
        attf[:, ti * ql * hd : (ti + 1) * ql * hd] = attr[ti]
    resid = tokens[pl.ds(pl.multiple_of(t * orow, orow), orow), :].astype(F32)
    hidden[...] = (dot(attf[...], wob[...]) + resid).astype(BF16)

    for i in range(1, PLANE):
        q = (p + i) % PLANE
        ref = fin.at[pl.ds(pl.multiple_of(q * prows, prows), prows), :]
        remote(ref, ref, dss.at[i], drs.at[q], other).wait_recv()
    got = fin[...]
    slot_col = got[:, cols : cols + 1].astype(F32)
    n = pack.shape[0]
    put = jnp.where(slot_col == (iota((n, rows), 1) + 1).astype(F32), 1.0, 0.0).astype(BF16)
    cache[...] = dot(got, put, 0, 0)[0:cols, :].astype(BF16)

    for i in range(1, PLANE):
        pcopy(i).wait_send()
    for i in range(1, TP):
        acopy(i).wait_send()


def per_device(tokens, norm_gain, q_gain, k_gain, w_query, w_keyval, w_out, lengths, cache_place):
    rows, width = tokens.shape
    seqs = lax.axis_size("seq")
    zn = seqs // PLANE
    hd = q_gain.shape[0]
    kvw = w_keyval.shape[1]
    cols = kvw // TP
    ql = w_query.shape[1] // hd
    cap = CAPACITY
    freq = (BASE ** (-(np.arange(hd // 2, dtype=np.float64) * 2.0) / hd)).astype(np.float32)
    vm = pl.BlockSpec(memory_space=pltpu.VMEM)
    hbm = pl.BlockSpec(memory_space=pl.ANY)
    packed = (seqs * cap, 256)
    dma = pltpu.SemaphoreType.DMA
    hidden, cache = pl.pallas_call(
        functools.partial(kernel, zn),
        out_shape=(
            jax.ShapeDtypeStruct((rows // TP, width), BF16),
            jax.ShapeDtypeStruct((cols, rows), BF16),
        ),
        in_specs=[vm] * 6 + [hbm] * 4,
        out_specs=(vm, vm),
        scratch_shapes=[
            pltpu.VMEM((rows, width), BF16),
            pltpu.VMEM((ql * hd, width), BF16),
            pltpu.VMEM((w_keyval.shape[0], kvw), BF16),
            pltpu.VMEM((kvw, w_keyval.shape[0]), BF16),
            pltpu.VMEM((4 * hd, width), BF16),
            pltpu.VMEM((3 * hd, width), BF16),
            pltpu.VMEM((w_out.shape[0] * TP, width), BF16),
            pltpu.VMEM((rows, width), BF16),
            pltpu.VMEM((3 * hd, rows), BF16),
            pltpu.VMEM((256, ql * rows), BF16),
            pltpu.VMEM((BACK + 1, PLANE, 2 * rows, 128), BF16),
            pltpu.VMEM((1, ql * rows), F32),
            pltpu.VMEM((1, ql * rows), F32),
            pltpu.VMEM((2 * hd, ql * rows), F32),
            pltpu.VMEM((rows, ql * hd), BF16),
            pltpu.VMEM((TP, rows // TP, ql * hd), BF16),
            pltpu.VMEM((rows // TP, TP * ql * hd), BF16),
            pltpu.VMEM(packed, BF16),
            pltpu.VMEM(packed, BF16),
            pltpu.VMEM(packed, BF16),
            pltpu.VMEM(packed, BF16),
            dma((4,)),
            dma((3, TP)),
            dma((3, TP)),
            dma((3, TP)),
            dma((3, TP)),
            pltpu.SemaphoreType.REGULAR((3, 2)),
            dma((1, 7)),
            dma((1, 7)),
            dma((BACK + 1, 9)),
            dma((BACK + 1, PLANE)),
            dma((BACK + 1,)),
            dma((BACK, 2)),
            dma((BACK + 1, 2)),
            dma((zn,)),
            dma((zn,)),
            dma((PLANE,)),
            dma((PLANE,)),
            dma((TP,)),
            dma((TP,)),
        ],
        compiler_params=pltpu.CompilerParams(
            collective_id=0, has_side_effects=True, vmem_limit_bytes=56 << 20
        ),
        name="layer",
    )(
        norm_gain.reshape(1, width),
        q_gain.reshape(1, hd),
        k_gain.reshape(1, hd),
        jnp.asarray(freq.reshape(-1, 1)),
        lengths.reshape(1, -1),
        cache_place.T,
        tokens,
        w_query.T,
        w_keyval,
        w_out,
    )
    return hidden, cache.T


CAPACITY = 4


def solution(mesh):
    placed = (
        P("seq", None),
        P(),
        P(),
        P(),
        P(None, "tp"),
        P("tp", None),
        P("tp", None),
        P(),
        P("seq", None),
    )
    return jax.shard_map(
        per_device,
        mesh=mesh,
        in_specs=placed,
        out_specs=(P(("seq", "tp"), None), P("seq", "tp")),
        check_vma=False,
    )
```
